128 devices in a mesh: stratum: 16 (over z, y_lo, core), replica: 8 (over x, y_hi).
Axes of the slice: x: 4, y: 4 (y_hi: 2, y_lo: 2; y = y_hi * 2 + y_lo), z: 4, core: 2. Of those that a mesh axis runs over, the one named last changes fastest.
Arguments:
- user_factors: float32 [524288, 128], P(('stratum', 'replica')), may hold values from -1.8 to 1.8
- item_factors: float32 [65536, 128], P('stratum'), may hold values from -1.8 to 1.8
- ratings: bfloat16 [2, 32768, 128, 128], P(None, ('stratum', 'replica')), may hold values from -9 to 9
- user_tile: int32 [2, 32768], P(None, ('stratum', 'replica')), may hold values from 0 to 31, as said below
- item_tile: int32 [2, 32768], P(None, ('stratum', 'replica')), may hold values from 0 to 31, as said below
- live_count: int32 [2, 128], P(None, ('stratum', 'replica')), may hold values from 64 to 256, as said below
- partner: int32 [16], replicated, may hold values from 0 to 15, as said below
Outputs:
- user_out: float32 [524288, 128], P(('stratum', 'replica'))
- item_out: float32 [65536, 128], P('stratum')
The draws below stay inside these ranges and needn't reach their ends.
Inputs may be any that keep to these rules, and one draw needn't show every extreme that they name: partner[i] = i XOR m for one m from 8 to 15, the same for every i. `user_tile`: within one device and one sub-epoch, its 256 slots name distinct pairs of user tile and item tile. `item_tile`: paired with user_tile as stated there. `live_count`: in every sub-epoch some device has all 256 slots live.
All inputs are finite; a program needn't handle non-finite values.
Results may differ from the reference program's by a relative error of at most 0.0012.
Values sent between devices are 32-bit elements; how exact they have to be, the bound alone decides.
A program may use at most 128 MiB of HBM per device.

```python
import jax
import jax.numpy as jnp
from jax import lax

RANK = 128
TILE = 128
USER_TILES = 32
ITEM_TILES = 32
TILE_SLOTS = 256
SUBEPOCHS = 2
USERS = 524288
ITEMS = 65536
TILES = 32768
N_STRATUM = 16
N_REPLICA = 8


def pick_slots(one_key):
    return jax.random.permutation(one_key, USER_TILES * ITEM_TILES)[:TILE_SLOTS]


def slot_pairs(key):
    base_key = jax.random.fold_in(key, 17)
    all_keys = jax.random.split(base_key, SUBEPOCHS * N_STRATUM * N_REPLICA)
    chosen = jax.vmap(pick_slots)(all_keys)
    return chosen.reshape(SUBEPOCHS, TILE_SLOTS * N_STRATUM * N_REPLICA).astype(jnp.int32)


def draw_user_tile(key, part):
    return (slot_pairs(key) // ITEM_TILES).astype(jnp.int32)


def draw_item_tile(key, part):
    return (slot_pairs(key) % ITEM_TILES).astype(jnp.int32)


def draw_live_count(key, part):
    devices_all = N_STRATUM * N_REPLICA
    lower_counts = jax.random.randint(jax.random.fold_in(key, 3), (SUBEPOCHS, devices_all), TILE_SLOTS // 4, TILE_SLOTS + 1)
    fullest = jax.random.randint(jax.random.fold_in(key, 5), (SUBEPOCHS, 1), 0, devices_all)
    positions = jnp.arange(devices_all, dtype=jnp.int32)[None, :]
    return jnp.where(positions == fullest, TILE_SLOTS, lower_counts).astype(jnp.int32)


def draw_partner(key, part):
    flip_mask = jax.random.randint(jax.random.fold_in(key, 9), (), N_STRATUM // 2, N_STRATUM)
    return jnp.bitwise_xor(jnp.arange(N_STRATUM, dtype=jnp.int32), flip_mask).astype(jnp.int32)


def levels(key, extent, pieces, smallest, top_value):
    level, own = 1.0, jax.random.fold_in(key, 6)
    for dim, parts in pieces:
        heights = jnp.exp(jax.random.uniform(jax.random.fold_in(own, dim), (parts,), jnp.float32, smallest / len(pieces), top_value / len(pieces)))
        level = level * jnp.repeat(heights, extent[dim] // parts).reshape([-1 if axis == dim else 1 for axis in range(len(extent))])
    return level


def scatter_about(key, extent, width, reach, pieces=(), kind=jnp.bfloat16):
    drawn = width * jax.random.normal(key, extent, jnp.float32)
    if pieces:
        drawn = drawn * levels(key, extent, pieces, -0.22, 0.18)
    return jnp.clip(drawn, -reach, reach).astype(kind)


def setup_inputs(seed: int = 0) -> dict:
    keys = jax.random.split(jax.random.key(seed), 8)
    return {
        "user_factors": scatter_about(keys[0], (USERS, RANK), 0.3, 1.8, ((0, 128),), jnp.float32),
        "item_factors": scatter_about(keys[1], (ITEMS, RANK), 0.3, 1.8, ((0, 16),), jnp.float32),
        "ratings": scatter_about(keys[2], (SUBEPOCHS, TILES, TILE, TILE), 1.5, 9.0, ((1, 128),)),
        "user_tile": draw_user_tile(jax.random.fold_in(keys[7], 71), 0),
        "item_tile": draw_item_tile(jax.random.fold_in(keys[7], 71), 0),
        "live_count": draw_live_count(jax.random.fold_in(keys[7], 71), 0),
        "partner": draw_partner(jax.random.fold_in(keys[7], 71), 0),
    }


LEARNING_RATE = 0.05
WEIGHT_DECAY = 0.05


def lowered(values):
    return lax.optimization_barrier(values.astype(jnp.bfloat16)).astype(jnp.float32)


def device_terms(user_rows, block_rows, rating_slots, user_index, item_index, slot_total):
    user_low = lowered(user_rows).reshape(USER_TILES, TILE, RANK)
    item_low = lowered(block_rows).reshape(ITEM_TILES, TILE, RANK)
    left_tiles = jnp.take(user_low, user_index, axis=0)
    right_tiles = jnp.take(item_low, item_index, axis=0)
    predicted = jnp.einsum("sik,sjk->sij", left_tiles, right_tiles)
    residual = lowered(rating_slots.astype(jnp.float32) - predicted)
    slot_user = jnp.einsum("sij,sjk->sik", residual, right_tiles)
    slot_item = jnp.einsum("sij,sik->sjk", residual, left_tiles)
    live_mask = (jnp.arange(TILE_SLOTS, dtype=jnp.int32) < slot_total).astype(jnp.float32)
    pick_user = (user_index[:, None] == jnp.arange(USER_TILES, dtype=jnp.int32)[None, :]).astype(jnp.float32) * live_mask[:, None]
    pick_item = (item_index[:, None] == jnp.arange(ITEM_TILES, dtype=jnp.int32)[None, :]).astype(jnp.float32) * live_mask[:, None]
    grad_user = jnp.einsum("sa,sik->aik", pick_user, slot_user, precision=lax.Precision.HIGHEST)
    grad_item = jnp.einsum("sa,sik->aik", pick_item, slot_item, precision=lax.Precision.HIGHEST)
    return (grad_user.reshape(USER_TILES * TILE, RANK), jnp.sum(pick_user, axis=0),
            grad_item.reshape(ITEM_TILES * TILE, RANK), jnp.sum(pick_item, axis=0))


def per_device(packed):
    return device_terms(*packed)


def reference(user_factors, item_factors, ratings, user_tile, item_tile, live_count, partner):
    devices_all = N_STRATUM * N_REPLICA
    user_rows = user_factors.reshape(devices_all, USER_TILES * TILE, RANK)
    blocks = item_factors.reshape(N_STRATUM, ITEM_TILES * TILE, RANK)
    for epoch_index in range(SUBEPOCHS):
        if epoch_index > 0:
            blocks = jnp.take(blocks, partner.astype(jnp.int32), axis=0)
        device_blocks = jnp.repeat(blocks, N_REPLICA, axis=0)
        grad_user, seen_user, grad_item, seen_item = lax.map(per_device, (
            user_rows, device_blocks,
            ratings[epoch_index].reshape(devices_all, TILE_SLOTS, TILE, TILE),
            user_tile[epoch_index].reshape(devices_all, TILE_SLOTS),
            item_tile[epoch_index].reshape(devices_all, TILE_SLOTS),
            live_count[epoch_index]))
        user_scale = jnp.repeat(jnp.maximum(seen_user, 1.0), TILE, axis=1)[:, :, None]
        user_rows = user_rows * (1.0 - LEARNING_RATE * WEIGHT_DECAY) + LEARNING_RATE * grad_user / user_scale
        stratum_grad = jnp.sum(grad_item.reshape(N_STRATUM, N_REPLICA, ITEM_TILES * TILE, RANK), axis=1)
        stratum_seen = jnp.sum(seen_item.reshape(N_STRATUM, N_REPLICA, ITEM_TILES), axis=1)
        item_scale = jnp.repeat(jnp.maximum(stratum_seen, 1.0), TILE, axis=1)[:, :, None]
        blocks = blocks * (1.0 - LEARNING_RATE * WEIGHT_DECAY) + LEARNING_RATE * stratum_grad / item_scale
    return user_rows.reshape(devices_all * USER_TILES * TILE, RANK), blocks.reshape(N_STRATUM * ITEM_TILES * TILE, RANK)
```

```python
import functools

import jax
import jax.numpy as jnp
from jax import lax
from jax.experimental import pallas as pl
from jax.experimental.pallas import tpu as pltpu
from jax.sharding import PartitionSpec as P

LR = 0.05
KEEP = 1.0 - 0.05*0.05
NT = (((1,), (1,)), ((), ()))
NN = (((1,), (0,)), ((), ()))
f32, bf16 = jnp.float32, jnp.bfloat16

def tile_kernel(epoch, slots, shards, chunks, group,
                ut, it, live_ref, users, items, ratings,
                users_out, grads_out,
                rat, uf, vf, ub, utb, vb, du, dv, su, si, rsem, msem):
    tiles = ub.shape[0]
    per = tiles // shards
    T = ub.shape[1]
    width = slots // chunks
    loads = [pltpu.make_async_copy(ratings.at[epoch, pl.ds(c*width, width)], rat.at[pl.ds(c*width, width)], rsem.at[c]) for c in range(chunks)]
    cu = pltpu.make_async_copy(users, uf, msem.at[0])
    cv = pltpu.make_async_copy(items, vf, msem.at[1])
    cu.start(); cv.start()
    for l in loads: l.start()

    @pl.loop(0, tiles)
    def _(b):
        su[b] = 0
        si[b] = 0
        du[b] = jnp.zeros((T, T), f32)
    @pl.loop(0, shards)
    def _(s):
        dv[s] = jnp.zeros(dv.shape[1:], f32)
    eye = (lax.broadcasted_iota(jnp.int32, (T, T), 0) == lax.broadcasted_iota(jnp.int32, (T, T), 1)).astype(bf16)
    cu.wait()
    @pl.loop(0, tiles, step=4)
    def _(b0):
        for k in range(4):
            b = b0 + k
            x = uf[pl.ds(b*T, T), :].astype(bf16)
            ub[b] = x
            utb[b] = lax.dot_general(eye, x, NT, preferred_element_type=f32).astype(bf16)
    cv.wait()
    @pl.loop(0, tiles, step=4)
    def _(b0):
        for k in range(4):
            b = b0 + k
            vb[b] = vf[pl.ds(b*T, T), :].astype(bf16)
    live = live_ref[epoch, 0]

    for c in range(chunks):
        loads[c].wait()
        base = c*width
        count = jnp.clip(live - base, 0, width)
        @pl.loop(0, pl.cdiv(count, group))
        def _(j):
            t0 = base + j*group
            aa, bb, rr = [], [], []
            for k in range(group):
                t = t0 + k
                a = ut[epoch, t]; b = it[epoch, t]
                aa.append(a); bb.append(b)
            for k in range(group):
                t = t0 + k
                p = lax.dot_general(ub[aa[k]], vb[bb[k]], NT, preferred_element_type=f32)
                r = rat[t].astype(f32) - p
                if k:
                    r = jnp.where(t < live, r, 0.0)
                rr.append(r.astype(bf16))
            gu = [lax.dot_general(rr[k], vb[bb[k]], NN, preferred_element_type=f32) for k in range(group)]
            gv = [lax.dot_general(utb[aa[k]], rr[k], NN, preferred_element_type=f32) for k in range(group)]
            for k in range(group):
                one = (t0 + k < live).astype(jnp.int32)
                du[aa[k]] += gu[k]
                s = bb[k] // per
                o = pl.multiple_of((bb[k] % per)*T, T)
                dv[s, pl.ds(o, T), :] += gv[k]
                su[aa[k]] = su[aa[k]] + one
                si[bb[k]] = si[bb[k]] + one
    row = lax.broadcasted_iota(jnp.int32, (8, T), 0)
    for s in range(shards):
        z = jnp.zeros((8, T), f32)
        for k in range(per):
            z = jnp.where(row == k, si[s*per+k].astype(f32), z)
        dv[s, pl.ds(per*T, 8), :] = z
    og = pltpu.make_async_copy(dv, grads_out, msem.at[2])
    og.start()
    @pl.loop(0, tiles, step=2)
    def _(b0):
        for k in range(2):
            b = b0 + k
            cnt = jnp.full((1, T), jnp.maximum(su[b], 1), jnp.int32).astype(f32)
            sl = pl.ds(pl.multiple_of(b*T, T), T)
            uf[sl, :] = uf[sl, :]*KEEP + du[b]*(LR/cnt)
    ou = pltpu.make_async_copy(uf, users_out, msem.at[3])
    ou.start()
    og.wait(); ou.wait()

def tiles_step(epoch, ut, it, live, users, items, ratings, shards=8, chunks=8, group=16):
    slots, T = ratings.shape[1], ratings.shape[2]
    tiles = users.shape[0]//T
    per = tiles//shards
    smem = pl.BlockSpec(memory_space=pltpu.SMEM)
    anyb = pl.BlockSpec(memory_space=pl.ANY)
    return pl.pallas_call(
        functools.partial(tile_kernel, epoch, slots, shards, chunks, group),
        out_shape=(jax.ShapeDtypeStruct(users.shape, f32), jax.ShapeDtypeStruct((shards, per*T+8, T), f32)),
        in_specs=[smem]*3+[anyb]*3, out_specs=(anyb, anyb),
        scratch_shapes=[pltpu.VMEM((slots,T,T),bf16), pltpu.VMEM(users.shape,f32), pltpu.VMEM(items.shape,f32),
            pltpu.VMEM((tiles,T,T),bf16),pltpu.VMEM((tiles,T,T),bf16),pltpu.VMEM((tiles,T,T),bf16),
            pltpu.VMEM((tiles,T,T),f32), pltpu.VMEM((shards,per*T+8,T),f32),
            pltpu.SMEM((tiles,),jnp.int32),pltpu.SMEM((tiles,),jnp.int32),
            pltpu.SemaphoreType.DMA((chunks,)), pltpu.SemaphoreType.DMA((4,))],
        compiler_params=pltpu.CompilerParams(vmem_limit_bytes=48<<20),
        name="tile_step",
    )(ut, it, live, users, items, ratings)


MESH = pl.DeviceIdType.MESH

def share_kernel(mask, n, grads, block, out, mine, parts, rows, incoming, s_rs, r_rs, s_ag, r_ag, s_ex, r_ex, lsem):
    s = lax.axis_index("stratum")
    r = lax.axis_index("replica")
    T = block.shape[1]
    height = rows.shape[0]
    bar = pltpu.get_barrier_semaphore()
    for k in range(1, n):
        pl.semaphore_signal(bar, inc=1, device_id=(s, lax.rem(r + k, n)), device_id_type=MESH)
    if mask:
        across = s + 0
        for bit in range(4):
            if mask >> bit & 1:
                across = across + (1 << bit) - 2 * (1 << bit) * (lax.rem(lax.div(s, 1 << bit), 2))
        pl.semaphore_signal(bar, inc=1, device_id=(across, r), device_id_type=MESH)
    cb = pltpu.make_async_copy(block.at[pl.ds(r * height, height)], rows, lsem.at[0])
    cb.start()
    cm = pltpu.make_async_copy(grads.at[r], mine, lsem.at[1])
    cm.start()
    pl.semaphore_wait(bar, n - 1 + (1 if mask else 0))
    outs = []
    for k in range(1, n):
        q = lax.rem(r + k, n)
        c = pltpu.make_async_remote_copy(src_ref=grads.at[q], dst_ref=parts.at[k - 1], send_sem=s_rs.at[k - 1], recv_sem=r_rs.at[k - 1], device_id=(s, q), device_id_type=MESH)
        c.start()
        outs.append(c)
    cm.wait()
    cb.wait()
    for k in range(n - 1):
        outs[k].wait_recv()
        mine[...] += parts[k]
    per = height // T
    for k in range(per):
        cnt = jnp.maximum(mine[pl.ds(height + k, 1), :], 1.0)
        sl = pl.ds(k * T, T)
        rows[sl, :] = rows[sl, :] * KEEP + mine[sl, :].T * (LR / cnt)
    if mask:
        ex = pltpu.make_async_remote_copy(src_ref=rows, dst_ref=incoming, send_sem=s_ex, recv_sem=r_ex, device_id=(across, r), device_id_type=MESH)
        ex.start()
        ex.wait()
        src = incoming
    else:
        src = rows
    lc = pltpu.make_async_copy(src, out.at[pl.ds(r * height, height)], lsem.at[0])
    lc.start()
    gs = []
    for k in range(1, n):
        q = lax.rem(r + k, n)
        c = pltpu.make_async_remote_copy(src_ref=src, dst_ref=out.at[pl.ds(r * height, height)], send_sem=s_ag.at[k - 1], recv_sem=r_ag.at[k - 1], device_id=(s, q), device_id_type=MESH)
        c.start()
        gs.append(c)
    for c in outs: c.wait_send()
    lc.wait()
    for c in gs: c.wait()


def share(grads, block, mask, cid, n):
    height = block.shape[0] // n
    anyb = pl.BlockSpec(memory_space=pl.ANY)
    T = block.shape[1]
    sems = lambda k: pltpu.SemaphoreType.DMA((k,))
    return pl.pallas_call(
        functools.partial(share_kernel, mask, n),
        out_shape=jax.ShapeDtypeStruct(block.shape, f32),
        in_specs=[anyb, anyb],
        out_specs=anyb,
        scratch_shapes=[
            pltpu.VMEM(grads.shape[1:], f32),
            pltpu.VMEM((n - 1, *grads.shape[1:]), f32),
            pltpu.VMEM((height, T), f32),
            pltpu.VMEM((height, T), f32),
            sems(n - 1), sems(n - 1), sems(n - 1), sems(n - 1),
            pltpu.SemaphoreType.DMA, pltpu.SemaphoreType.DMA, sems(2),
        ],
        compiler_params=pltpu.CompilerParams(collective_id=cid, has_side_effects=True),
        name=f"share_{mask}",
    )(grads, block)


def local(user_factors, item_factors, ratings, user_tile, item_tile, live_count, partner):
    n = lax.axis_size("replica")
    half = lax.axis_size("stratum") // 2
    users, grads = tiles_step(0, user_tile, item_tile, live_count, user_factors, item_factors, ratings, n)
    branches = [functools.partial(share, mask=half + k, cid=1 + k, n=n) for k in range(half)]
    block = lax.switch(partner[0] - half, branches, grads, item_factors)
    users, grads = tiles_step(1, user_tile, item_tile, live_count, users, block, ratings, n)
    return users, share(grads, block, 0, 0, n)


def solution(mesh):
    return jax.shard_map(
        local,
        mesh=mesh,
        in_specs=(
            P(("stratum", "replica"), None),
            P("stratum", None),
            P(None, ("stratum", "replica"), None, None),
            P(None, ("stratum", "replica")),
            P(None, ("stratum", "replica")),
            P(None, ("stratum", "replica")),
            P(),
        ),
        out_specs=(P(("stratum", "replica"), None), P("stratum", None)),
        check_vma=False,
    )
```

```python
import functools

import jax
import jax.numpy as jnp
from jax import lax
from jax.experimental import pallas as pl
from jax.experimental.pallas import tpu as pltpu
from jax.sharding import PartitionSpec as P

LR = 0.05
KEEP = 1.0 - 0.05*0.05
NT = (((1,), (1,)), ((), ()))
NN = (((1,), (0,)), ((), ()))
f32, bf16 = jnp.float32, jnp.bfloat16

def tile_kernel(epoch, slots, shards, chunks, group,
                ut, it, live_ref, users, items, ratings,
                users_out, grads_out, counts_out,
                rat, uf, vf, ub, utb, vb, du, dv, cv_, su, si, rsem, msem):
    tiles = ub.shape[0]
    T = ub.shape[1]
    width = slots // chunks
    loads = [pltpu.make_async_copy(ratings.at[epoch, pl.ds(c*width, width)], rat.at[pl.ds(c*width, width)], rsem.at[c]) for c in range(chunks)]
    cu = pltpu.make_async_copy(users, uf, msem.at[0])
    cv = pltpu.make_async_copy(items, vf, msem.at[1])
    cu.start(); cv.start()
    for l in loads: l.start()

    @pl.loop(0, tiles)
    def _(b):
        su[b] = 0
        si[b] = 0
        du[b] = jnp.zeros((T, T), f32)
        dv[b] = jnp.zeros((T, T), f32)
    eye = (lax.broadcasted_iota(jnp.int32, (T, T), 0) == lax.broadcasted_iota(jnp.int32, (T, T), 1)).astype(bf16)
    cu.wait()
    @pl.loop(0, tiles, step=4)
    def _(b0):
        for k in range(4):
            b = b0 + k
            x = uf[pl.ds(b*T, T), :].astype(bf16)
            ub[b] = x
            utb[b] = lax.dot_general(eye, x, NT, preferred_element_type=f32).astype(bf16)
    cv.wait()
    @pl.loop(0, tiles, step=4)
    def _(b0):
        for k in range(4):
            b = b0 + k
            vb[b] = vf[pl.ds(b*T, T), :].astype(bf16)
    live = live_ref[epoch, 0]

    for c in range(chunks):
        loads[c].wait()
        base = c*width
        count = jnp.clip(live - base, 0, width)
        @pl.loop(0, pl.cdiv(count, group))
        def _(j):
            t0 = base + j*group
            aa, bb, rr = [], [], []
            for k in range(group):
                t = t0 + k
                a = ut[epoch, t]; b = it[epoch, t]
                aa.append(a); bb.append(b)
            for k in range(group):
                t = t0 + k
                p = lax.dot_general(ub[aa[k]], vb[bb[k]], NT, preferred_element_type=f32)
                r = rat[t].astype(f32) - p
                if k:
                    r = jnp.where(t < live, r, 0.0)
                rr.append(r.astype(bf16))
            gu = [lax.dot_general(rr[k], vb[bb[k]], NN, preferred_element_type=f32) for k in range(group)]
            gv = [lax.dot_general(utb[aa[k]], rr[k], NN, preferred_element_type=f32) for k in range(group)]
            for k in range(group):
                one = (t0 + k < live).astype(jnp.int32)
                du[aa[k]] += gu[k]
                dv[bb[k]] += gv[k]
                su[aa[k]] = su[aa[k]] + one
                si[bb[k]] = si[bb[k]] + one
    row = lax.broadcasted_iota(jnp.int32, (8, T), 0)
    for r in range(shards):
        x, hy = r // 2, r % 2
        lo, hi = x % 2, x // 2
        z = jnp.zeros((8, T), f32)
        for d in range(2):
            for c in range(2):
                b = (d*2+c)*8 + (hi if d else lo ^ hi)*4 + hy*2 + lo
                z = jnp.where(row == d*2+c, si[b].astype(f32), z)
        cv_[r] = z
    oc = pltpu.make_async_copy(cv_, counts_out, msem.at[4])
    oc.start()
    og = pltpu.make_async_copy(dv, grads_out, msem.at[2])
    og.start()
    @pl.loop(0, tiles, step=2)
    def _(b0):
        for k in range(2):
            b = b0 + k
            cnt = jnp.full((1, T), jnp.maximum(su[b], 1), jnp.int32).astype(f32)
            sl = pl.ds(pl.multiple_of(b*T, T), T)
            uf[sl, :] = uf[sl, :]*KEEP + du[b]*(LR/cnt)
    ou = pltpu.make_async_copy(uf, users_out, msem.at[3])
    ou.start()
    og.wait(); ou.wait(); oc.wait()

def tiles_step(epoch, ut, it, live, users, items, ratings, shards=8, chunks=8, group=16):
    slots, T = ratings.shape[1], ratings.shape[2]
    tiles = users.shape[0]//T
    smem = pl.BlockSpec(memory_space=pltpu.SMEM)
    anyb = pl.BlockSpec(memory_space=pl.ANY)
    return pl.pallas_call(
        functools.partial(tile_kernel, epoch, slots, shards, chunks, group),
        out_shape=(jax.ShapeDtypeStruct(users.shape, f32), jax.ShapeDtypeStruct((tiles, T, T), f32), jax.ShapeDtypeStruct((shards, 8, T), f32)),
        in_specs=[smem]*3+[anyb]*3, out_specs=(anyb,)*3,
        scratch_shapes=[pltpu.VMEM((slots,T,T),bf16), pltpu.VMEM(users.shape,f32), pltpu.VMEM(items.shape,f32),
            pltpu.VMEM((tiles,T,T),bf16),pltpu.VMEM((tiles,T,T),bf16),pltpu.VMEM((tiles,T,T),bf16),
            pltpu.VMEM((tiles,T,T),f32), pltpu.VMEM((tiles,T,T),f32), pltpu.VMEM((shards,8,T),f32),
            pltpu.SMEM((tiles,),jnp.int32),pltpu.SMEM((tiles,),jnp.int32),
            pltpu.SemaphoreType.DMA((chunks,)), pltpu.SemaphoreType.DMA((5,))],
        compiler_params=pltpu.CompilerParams(vmem_limit_bytes=48<<20),
        name="tile_step",
    )(ut, it, live, users, items, ratings)


MESH = pl.DeviceIdType.MESH


def share_kernel(mask, grads, counts, block, out, acc, old, new, rx1, ry, rx2, cin, cmine,
                 s1, r1, sy, ry_s, s2, r2, sc, rc, se, re, t2, q2, ty, qy, t1, q1, lsem):
    T = block.shape[1]
    n = counts.shape[0]
    s = lax.axis_index("stratum")
    r = lax.axis_index("replica")
    x, hy = lax.div(r, 2), lax.rem(r, 2)
    lo, hi = lax.rem(x, 2), lax.div(x, 2)
    xa = x + 1 - 2 * lo
    xb = 3 - x
    at = lambda x_, y_: (s, x_ * 2 + y_)
    first = (at(xa, hy), at(xb, hy))
    second = (at(xb, hy), at(xa, hy))
    over = at(x, 1 - hy)
    h1 = (lo + hi - 2 * lo * hi, hi)
    h2 = (lo, lo)

    def tile(d, c, a, b, e):
        return (d * 2 + c) * 8 + a * 4 + b * 2 + e

    def put(src, dst, ss, rs, dev):
        cp = pltpu.make_async_remote_copy(src_ref=src, dst_ref=dst, send_sem=ss, recv_sem=rs, device_id=dev, device_id_type=MESH)
        cp.start()
        return cp

    def rows(b):
        return pl.ds(pl.multiple_of(b * T, T), T)

    bar = pltpu.get_barrier_semaphore()
    for k in range(1, n):
        pl.semaphore_signal(bar, inc=1, device_id=(s, lax.rem(r + k, n)), device_id_type=MESH)
    across = s
    if mask:
        for bit in range(4):
            if mask >> bit & 1:
                across = across + (1 << bit) - (2 << bit) * lax.rem(lax.div(s, 1 << bit), 2)
        pl.semaphore_signal(bar, inc=1, device_id=(across, r), device_id_type=MESH)
    local = [pltpu.make_async_copy(grads, acc, lsem.at[0]), pltpu.make_async_copy(counts.at[r], cmine, lsem.at[1])]
    mine = {}
    for d in range(2):
        for c in range(2):
            b = tile(d, c, h1[d], hy, h2[d])
            mine[d, c] = b
            local.append(pltpu.make_async_copy(block.at[rows(b)], old.at[d, c], lsem.at[2 + d * 2 + c]))
    for cp in local:
        cp.start()
    pl.semaphore_wait(bar, n - 1 + (1 if mask else 0))

    pend = []
    got1, goty, got2, gote = {}, {}, {}, {}
    for half in range(2):
        for c in range(2):
            for e in range(2):
                for d in range(2):
                    i = half * 2 + e
                    yb = hy if half else 1 - hy
                    eb = 1 - h2[d] if e else h2[d]
                    got1[d, c, i] = put(grads.at[tile(d, c, 1 - h1[d], yb, eb)], rx1.at[d, c, i], s1.at[d, c, i], r1.at[d, c, i], first[d])
        if not half:
            gotc = [put(counts.at[lax.rem(r + k, n)], cin.at[k - 1], sc.at[k - 1], rc.at[k - 1], (s, lax.rem(r + k, n))) for k in range(1, n)]
    for cp in local:
        cp.wait()

    def add(d, c, a, b, e, part):
        acc[tile(d, c, a, b, e)] += part[...]

    def take1(c, i):
        for d in range(2):
            e = h2[d] if i % 2 else 1 - h2[d]
            b = hy if i >= 2 else 1 - hy
            got1[d, c, i].wait_recv()
            add(d, c, h1[d], b, e, rx1.at[d, c, i])
            if i < 2:
                goty[d, c, i] = put(acc.at[tile(d, c, h1[d], b, e)], ry.at[d, c, i], sy.at[d, c, i], ry_s.at[d, c, i], over)

    def takey(c, j):
        for d in range(2):
            e = h2[d] if j else 1 - h2[d]
            goty[d, c, j].wait_recv()
            add(d, c, h1[d], hy, e, ry.at[d, c, j])
            if j == 0:
                got2[d, c] = put(acc.at[tile(d, c, h1[d], hy, e)], rx2.at[d, c], s2.at[d, c], r2.at[d, c], second[d])

    own = {}
    def finish(c):
        for d in range(2):
            b = mine[d, c]
            got2[d, c].wait_recv()
            total = acc[b] + rx2[d, c]
            cnt = jnp.maximum(cmine[pl.ds(d * 2 + c, 1), :], 1.0)
            fresh = old[d, c] * KEEP + total.T * (LR / cnt)
            if mask:
                new[d, c] = fresh
                gote[d, c] = put(new.at[d, c], out.at[rows(b)], se.at[d, c], re.at[d, c], (across, r))
            else:
                out[rows(b), :] = fresh

    ag2, agy, ag1 = {}, {}, {}

    def send2(d, c, b):
        ag2[d, c] = put(out.at[rows(b)], out.at[rows(b)], t2.at[d, c], q2.at[d, c], second[d])

    def sendy(d, c, j, b):
        agy[d, c, j] = put(out.at[rows(b)], out.at[rows(b)], ty.at[d, c, j], qy.at[d, c, j], over)

    def send1(d, c, i, b):
        ag1[d, c, i] = put(out.at[rows(b)], out.at[rows(b)], t1.at[d, c, i], q1.at[d, c, i], first[d])

    def spread(c):
        for d in range(2):
            b = mine[d, c]
            if mask:
                gote[d, c].wait_recv()
            send2(d, c, b)
            sendy(d, c, 0, b)
            send1(d, c, 0, b)

    def pass2(c):
        for d in range(2):
            ag2[d, c].wait_recv()
            b = tile(d, c, h1[d], hy, 1 - h2[d])
            sendy(d, c, 1, b)
            send1(d, c, 1, b)

    def passy(c, j):
        for d in range(2):
            agy[d, c, j].wait_recv()
            b = tile(d, c, h1[d], 1 - hy, 1 - h2[d] if j else h2[d])
            send1(d, c, 2 + j, b)

    for c in range(2):
        take1(c, 0)
        take1(c, 1)
    for g in gotc:
        g.wait_recv()
    cmine[...] += functools.reduce(lambda p, q: p + q, [cin[k] for k in range(n - 1)])
    take1(0, 2)
    take1(0, 3)
    takey(0, 0)
    takey(0, 1)
    take1(1, 2)
    finish(0)
    take1(1, 3)
    takey(1, 0)
    spread(0)
    takey(1, 1)
    finish(1)
    pass2(0)
    passy(0, 0)
    spread(1)
    passy(0, 1)
    pass2(1)
    passy(1, 0)
    passy(1, 1)
    for table in (got1, goty, got2, gote):
        for cp in table.values():
            cp.wait_send()
    for g in gotc:
        g.wait_send()
    for table in (ag2, agy):
        for cp in table.values():
            cp.wait_send()
    for cp in ag1.values():
        cp.wait()


def share(grads, counts, block, mask, cid):
    tiles, T = grads.shape[0], grads.shape[1]
    n = counts.shape[0]
    anyb = pl.BlockSpec(memory_space=pl.ANY)
    dma = lambda *k: pltpu.SemaphoreType.DMA(k)
    both = lambda *k: [dma(*k), dma(*k)]
    return pl.pallas_call(
        functools.partial(share_kernel, mask),
        out_shape=pltpu.VMEM(block.shape, f32),
        in_specs=[anyb] * 3,
        out_specs=pl.BlockSpec(memory_space=pltpu.VMEM),
        scratch_shapes=[
            pltpu.VMEM((tiles, T, T), f32),
            pltpu.VMEM((2, 2, T, T), f32),
            pltpu.VMEM((2, 2, T, T), f32),
            pltpu.VMEM((2, 2, 4, T, T), f32),
            pltpu.VMEM((2, 2, 2, T, T), f32),
            pltpu.VMEM((2, 2, T, T), f32),
            pltpu.VMEM((n - 1, 8, T), f32),
            pltpu.VMEM((8, T), f32),
            *both(2, 2, 4), *both(2, 2, 2), *both(2, 2), *both(n - 1), *both(2, 2),
            *both(2, 2), *both(2, 2, 2), *both(2, 2, 4), dma(6),
        ],
        compiler_params=pltpu.CompilerParams(collective_id=cid, has_side_effects=True, vmem_limit_bytes=24 << 20),
        name=f"share_{mask}",
    )(grads, counts, block)


def local(user_factors, item_factors, ratings, user_tile, item_tile, live_count, partner):
    n = lax.axis_size("replica")
    half = lax.axis_size("stratum") // 2
    users, grads, counts = tiles_step(0, user_tile, item_tile, live_count, user_factors, item_factors, ratings, n)
    branches = [functools.partial(share, mask=half + k, cid=1 + k) for k in range(half)]
    block = lax.switch(partner[0] - half, branches, grads, counts, item_factors)
    users, grads, counts = tiles_step(1, user_tile, item_tile, live_count, users, block, ratings, n)
    return users, share(grads, counts, block, 0, 0)


def solution(mesh):
    return jax.shard_map(
        local,
        mesh=mesh,
        in_specs=(
            P(("stratum", "replica"), None),
            P("stratum", None),
            P(None, ("stratum", "replica"), None, None),
            P(None, ("stratum", "replica")),
            P(None, ("stratum", "replica")),
            P(None, ("stratum", "replica")),
            P(),
        ),
        out_specs=(P(("stratum", "replica"), None), P("stratum", None)),
        check_vma=False,
    )
```

```python
import functools

import jax
import jax.numpy as jnp
from jax import lax
from jax.experimental import pallas as pl
from jax.experimental.pallas import tpu as pltpu
from jax.sharding import PartitionSpec as P

LR = 0.05
KEEP = 1.0 - 0.05 * 0.05
NT = (((1,), (1,)), ((), ()))
NN = (((1,), (0,)), ((), ()))
f32, bf16, i32 = jnp.float32, jnp.bfloat16, jnp.int32
GROUP = 16


def pin(x, space=pltpu.HBM):
    return pltpu.with_memory_space_constraint(x, space)


def tile_kernel(epoch, shards, chunks, ut_in, it_in, live_in, users, items, ratings,
                users_out, dv, counts_out,
                ut, it, live_ref, rat, uf, vf, ub, utb, vb, du,
                rbuf, pa, p1, p2, nb, pend, su, si, rsem, msem, osem):
    tiles, T = ub.shape[0], ub.shape[1]
    slots = rat.shape[0]
    width = slots // chunks
    first = epoch == 0
    per = slots // tiles

    def load(c):
        o = pl.ds(c * width, width)
        return pltpu.make_async_copy(ratings.at[epoch, o], rat.at[o], rsem.at[c])

    def rows(b):
        return pl.ds(pl.multiple_of(b * T, T), T)

    small = [pltpu.make_async_copy(ut_in, ut, msem.at[0]), pltpu.make_async_copy(it_in, it, msem.at[1]),
             pltpu.make_async_copy(live_in, live_ref, msem.at[2])]
    big = [pltpu.make_async_copy(users, uf, msem.at[3]), pltpu.make_async_copy(items, vf, msem.at[4])]
    for cp in small + big:
        cp.start()
    for c in range(chunks):
        load(c).start()

    @pl.loop(0, tiles)
    def _(b):
        su[b] = 0
        si[b] = 0
        pend[b] = -1
        du[b] = jnp.zeros((T, T), f32)
        dv[b] = jnp.zeros((T, T), f32)

    for cp in small + big:
        cp.wait()
    live = live_ref[epoch, 0]
    eye = (lax.broadcasted_iota(i32, (T, T), 0) == lax.broadcasted_iota(i32, (T, T), 1)).astype(bf16)

    @functools.partial(lax.fori_loop, 0, tiles // 2, init_val=jnp.int32(GROUP))
    def pairs(i, np):
        for k in range(2):
            b = i * 2 + k
            x = uf[rows(b), :].astype(bf16)
            ub[b] = x
            utb[b] = lax.dot_general(eye, x, NT, preferred_element_type=f32).astype(bf16)
            vb[b] = vf[rows(b), :].astype(bf16)
        for k in range(2 * per):
            t = i * (2 * per) + k
            a, b = ut[epoch, t], it[epoch, t]
            valid = t < live
            q = pend[a]
            has = jnp.logical_and(valid, q >= 0)
            pa[np] = a
            p1[np] = q
            p2[np] = t
            np = np + has.astype(i32)
            pend[a] = jnp.where(valid, jnp.where(has, -1, t), q)
            one = valid.astype(i32)
            su[a] = su[a] + one
            si[b] = si[b] + one
        nb[i] = np
        return np

    @functools.partial(lax.fori_loop, 0, tiles, init_val=pairs)
    def total(a, np):
        q = pend[a]
        pa[np] = a
        p1[np] = q
        p2[np] = -1
        return np + (q >= 0).astype(i32)

    for k in range(GROUP):
        for o in (0, total):
            pa[o + k] = 0
            p1[o + k] = -1
            p2[o + k] = -1

    rbuf[...] = jnp.zeros(rbuf.shape, bf16)

    def names(g):
        out = []
        for k in range(GROUP):
            p = g * GROUP + k
            x, y = p1[p], p2[p]
            tx, ty = jnp.maximum(x, 0), jnp.maximum(y, 0)
            out.append((pa[p], x, y, tx, ty, it[epoch, tx], it[epoch, ty]))
        return out

    def flush(g):
        todo = names(g)
        gu, gv = [], []
        for k, (a, x, y, tx, ty, bx, by) in enumerate(todo):
            r = rbuf[k]
            v = jnp.concatenate([vb[bx], vb[by]], axis=0)
            gu.append(lax.dot_general(r, v, NN, preferred_element_type=f32))
            gv.append(lax.dot_general(utb[a], r, NN, preferred_element_type=f32))
        return todo, gu, gv

    def fill(g):
        res = []
        for k, (a, x, y, tx, ty, bx, by) in enumerate(names(g)):
            v = jnp.concatenate([vb[bx], vb[by]], axis=0)
            p = lax.dot_general(ub[a], v, NT, preferred_element_type=f32)
            r1 = (rat[tx].astype(f32) - p[:, :T]).astype(bf16)
            r2 = (rat[ty].astype(f32) - p[:, T:]).astype(bf16)
            zero = jnp.zeros((T, T), bf16)
            res.append(jnp.concatenate([jnp.where(x >= 0, r1, zero), jnp.where(y >= 0, r2, zero)], axis=1))
        return res

    def settle(todo, gu, gv):
        for k, (a, x, y, tx, ty, bx, by) in enumerate(todo):
            du[a] += gu[k]
            dv[bx] += gv[k][:, :T]
            dv[by] += gv[k][:, T:]

    def work(g, carry):
        todo, gu, gv = flush(g)
        res = fill(g + 1)
        for k in range(GROUP):
            rbuf[k] = res[k]
        settle(todo, gu, gv)
        return carry

    def chunk(c, done):
        load(c).wait()
        upto = nb[(c + 1) * (tiles // 2 // chunks) - 1] // GROUP - 1
        upto = jnp.where(c == chunks - 1, pl.cdiv(total, GROUP) - 1, upto)
        lax.fori_loop(done, upto, work, 0)
        return jnp.maximum(done, upto)

    ended = lax.fori_loop(0, chunks, chunk, jnp.int32(0))
    settle(*flush(ended))

    row = lax.broadcasted_iota(i32, (8, T), 0)
    for r in range(shards):
        x, hy = r // 2, r % 2
        lo, hi = x % 2, x // 2
        z = jnp.zeros((8, T), f32)
        for d in range(2):
            for c in range(2):
                b = (d * 2 + c) * 8 + (hi if d else lo ^ hi) * 4 + hy * 2 + lo
                z = jnp.where(row == d * 2 + c, si[b].astype(f32), z)
        counts_out[r] = z


    def update(i, carry):
        for k in range(2):
            b = i * 2 + k
            cnt = jnp.full((1, T), jnp.maximum(su[b], 1), i32).astype(f32)
            uf[rows(b), :] = uf[rows(b), :] * KEEP + du[b] * (LR / cnt)
        return carry

    quarter = tiles // 4
    sent = []
    for part in range(4):
        lax.fori_loop(part * quarter // 2, (part + 1) * quarter // 2, update, 0)
        o = pl.ds(part * quarter * T, quarter * T)
        sent.append(pltpu.make_async_copy(uf.at[o], users_out.at[o], osem.at[part]))
        sent[-1].start()
    for cp in sent:
        cp.wait()


def tiles_step(epoch, ut, it, live, users, items, ratings, shards=8, chunks=8):
    slots, T = ratings.shape[1], ratings.shape[2]
    tiles = users.shape[0] // T
    first = epoch == 0
    hbm = pl.BlockSpec(memory_space=pltpu.HBM)
    vmem = pl.BlockSpec(memory_space=pltpu.VMEM)
    smem = lambda *k: pltpu.SMEM(k, i32)
    length = slots // 2 + tiles + 2 * GROUP
    return pl.pallas_call(
        functools.partial(tile_kernel, epoch, shards, chunks),
        out_shape=(pltpu.HBM(users.shape, f32), pltpu.VMEM((tiles, T, T), f32), pltpu.VMEM((shards, 8, T), f32)),
        in_specs=[hbm] * 4 + [hbm if first else pl.BlockSpec(memory_space=pl.ANY)] + [hbm],
        out_specs=(hbm, vmem, vmem),
        scratch_shapes=[
            smem(*ut.shape), smem(*it.shape), smem(*live.shape),
            pltpu.VMEM((slots, T, T), bf16),
            pltpu.VMEM(users.shape, f32),
            pltpu.VMEM(items.shape, f32),
            pltpu.VMEM((tiles, T, T), bf16), pltpu.VMEM((tiles, T, T), bf16), pltpu.VMEM((tiles, T, T), bf16),
            pltpu.VMEM((tiles, T, T), f32),
            pltpu.VMEM((GROUP, T, 2 * T), bf16),
            smem(length), smem(length), smem(length), smem(tiles // 2), smem(tiles), smem(tiles), smem(tiles),
            pltpu.SemaphoreType.DMA((chunks,)), pltpu.SemaphoreType.DMA((5,)), pltpu.SemaphoreType.DMA((4,)),
        ],
        compiler_params=pltpu.CompilerParams(vmem_limit_bytes=32 << 20),
        name=f"tile_step_{epoch}",
    )(pin(ut), pin(it), pin(live), pin(users), pin(items) if first else items, pin(ratings))


MESH = pl.DeviceIdType.MESH


def share_kernel(mask, grads, counts, block, dest, hold, acc, old, new, rx1, ry, rx2, cin, cmine,
                 s1, r1, sy, ry_s, s2, r2, sc, rc, se, re, t2, q2, ty, qy, t1, q1, lsem, wsem):
    T = block.shape[1]
    n = counts.shape[0]
    s = lax.axis_index("stratum")
    r = lax.axis_index("replica")
    x, hy = lax.div(r, 2), lax.rem(r, 2)
    lo, hi = lax.rem(x, 2), lax.div(x, 2)
    xa = x + 1 - 2 * lo
    xb = 3 - x
    at = lambda x_, y_: (s, x_ * 2 + y_)
    first = (at(xa, hy), at(xb, hy))
    second = (at(xb, hy), at(xa, hy))
    over = at(x, 1 - hy)
    h1 = (lo + hi - 2 * lo * hi, hi)
    h2 = (lo, lo)

    def tile(d, c, a, b, e):
        return (d * 2 + c) * 8 + a * 4 + b * 2 + e

    def put(src, dst, ss, rs, dev):
        cp = pltpu.make_async_remote_copy(src_ref=src, dst_ref=dst, send_sem=ss, recv_sem=rs, device_id=dev, device_id_type=MESH)
        cp.start()
        return cp

    def rows(b):
        return pl.ds(pl.multiple_of(b * T, T), T)

    out = hold if mask else dest
    saved = []

    def save(b):
        if mask:
            saved.append(pltpu.make_async_copy(out.at[rows(b)], dest.at[rows(b)], wsem.at[len(saved)]))
            saved[-1].start()

    bar = pltpu.get_barrier_semaphore()
    for k in range(1, n):
        pl.semaphore_signal(bar, inc=1, device_id=(s, lax.rem(r + k, n)), device_id_type=MESH)
    across = s
    if mask:
        for bit in range(4):
            if mask >> bit & 1:
                across = across + (1 << bit) - (2 << bit) * lax.rem(lax.div(s, 1 << bit), 2)
        pl.semaphore_signal(bar, inc=1, device_id=(across, r), device_id_type=MESH)
    local = [pltpu.make_async_copy(counts.at[r], cmine, lsem.at[1])]
    mine = {}
    for d in range(2):
        for c in range(2):
            b = tile(d, c, h1[d], hy, h2[d])
            mine[d, c] = b
            local.append(pltpu.make_async_copy(block.at[rows(b)], old.at[d, c], lsem.at[2 + d * 2 + c]))
    for cp in local:
        cp.start()
    pl.semaphore_wait(bar, n - 1 + (1 if mask else 0))

    pend = []
    got1, goty, got2, gote = {}, {}, {}, {}
    for half in range(2):
        for c in range(2):
            for e in range(2):
                for d in range(2):
                    i = half * 2 + e
                    yb = hy if half else 1 - hy
                    eb = 1 - h2[d] if e else h2[d]
                    got1[d, c, i] = put(grads.at[tile(d, c, 1 - h1[d], yb, eb)], rx1.at[d, c, i], s1.at[d, c, i], r1.at[d, c, i], first[d])
        if not half:
            gotc = [put(counts.at[lax.rem(r + k, n)], cin.at[k - 1], sc.at[k - 1], rc.at[k - 1], (s, lax.rem(r + k, n))) for k in range(1, n)]
    for cp in local:
        cp.wait()

    def add(d, c, a, b, e, part):
        t = tile(d, c, a, b, e)
        acc[t] = acc[t] + part[...]

    def take1(c, i):
        for d in range(2):
            e = h2[d] if i % 2 else 1 - h2[d]
            b = hy if i >= 2 else 1 - hy
            got1[d, c, i].wait_recv()
            t = tile(d, c, h1[d], b, e)
            acc[t] = grads[t] + rx1[d, c, i]
            if i < 2:
                goty[d, c, i] = put(acc.at[tile(d, c, h1[d], b, e)], ry.at[d, c, i], sy.at[d, c, i], ry_s.at[d, c, i], over)

    def takey(c, j):
        for d in range(2):
            e = h2[d] if j else 1 - h2[d]
            goty[d, c, j].wait_recv()
            add(d, c, h1[d], hy, e, ry.at[d, c, j])
            if j == 0:
                got2[d, c] = put(acc.at[tile(d, c, h1[d], hy, e)], rx2.at[d, c], s2.at[d, c], r2.at[d, c], second[d])

    own = {}
    def finish(c):
        for d in range(2):
            b = mine[d, c]
            got2[d, c].wait_recv()
            total = acc[b] + rx2[d, c]
            cnt = jnp.maximum(cmine[pl.ds(d * 2 + c, 1), :], 1.0)
            fresh = old[d, c] * KEEP + total.T * (LR / cnt)
            if mask:
                new[d, c] = fresh
                gote[d, c] = put(new.at[d, c], out.at[rows(b)], se.at[d, c], re.at[d, c], (across, r))
            else:
                out[rows(b), :] = fresh

    ag2, agy, ag1 = {}, {}, {}

    def send2(d, c, b):
        ag2[d, c] = put(out.at[rows(b)], out.at[rows(b)], t2.at[d, c], q2.at[d, c], second[d])

    def sendy(d, c, j, b):
        agy[d, c, j] = put(out.at[rows(b)], out.at[rows(b)], ty.at[d, c, j], qy.at[d, c, j], over)

    def send1(d, c, i, b):
        ag1[d, c, i] = put(out.at[rows(b)], out.at[rows(b)], t1.at[d, c, i], q1.at[d, c, i], first[d])

    def spread(c):
        for d in range(2):
            b = mine[d, c]
            if mask:
                gote[d, c].wait_recv()
            send2(d, c, b)
            sendy(d, c, 0, b)
            send1(d, c, 0, b)
            save(b)

    def pass2(c):
        for d in range(2):
            ag2[d, c].wait_recv()
            b = tile(d, c, h1[d], hy, 1 - h2[d])
            sendy(d, c, 1, b)
            send1(d, c, 1, b)
            save(b)

    def passy(c, j):
        for d in range(2):
            agy[d, c, j].wait_recv()
            b = tile(d, c, h1[d], 1 - hy, 1 - h2[d] if j else h2[d])
            send1(d, c, 2 + j, b)
            save(b)

    for c in range(2):
        take1(c, 0)
        take1(c, 1)
    for g in gotc:
        g.wait_recv()
    cmine[...] += functools.reduce(lambda p, q: p + q, [cin[k] for k in range(n - 1)])
    take1(0, 2)
    take1(0, 3)
    takey(0, 0)
    takey(0, 1)
    take1(1, 2)
    finish(0)
    take1(1, 3)
    takey(1, 0)
    spread(0)
    takey(1, 1)
    finish(1)
    pass2(0)
    passy(0, 0)
    spread(1)
    passy(0, 1)
    pass2(1)
    passy(1, 0)
    passy(1, 1)
    for c in range(2):
        for i in range(4):
            for d in range(2):
                ag1[d, c, i].wait_recv()
                save(tile(d, c, 1 - h1[d], 1 - hy if i >= 2 else hy, h2[d] if i % 2 else 1 - h2[d]))
    for table in (got1, goty, got2, gote, ag2, agy, ag1):
        for cp in table.values():
            cp.wait_send()
    for g in gotc:
        g.wait_send()
    for cp in saved:
        cp.wait()


def share(grads, counts, block, mask, cid):
    tiles, T = grads.shape[0], grads.shape[1]
    n = counts.shape[0]
    vmem = pl.BlockSpec(memory_space=pltpu.VMEM)
    hbm = pl.BlockSpec(memory_space=pltpu.HBM)
    dma = lambda *k: pltpu.SemaphoreType.DMA(k)
    both = lambda *k: [dma(*k), dma(*k)]
    return pl.pallas_call(
        functools.partial(share_kernel, mask),
        out_shape=(pltpu.HBM if mask else pltpu.VMEM)(block.shape, f32),
        in_specs=[vmem, vmem, hbm if mask else pl.BlockSpec(memory_space=pl.ANY)],
        out_specs=hbm if mask else vmem,
        scratch_shapes=[
            pltpu.VMEM(block.shape if mask else (8, T), f32),
            pltpu.VMEM((tiles, T, T), f32),
            pltpu.VMEM((2, 2, T, T), f32),
            pltpu.VMEM((2, 2, T, T), f32),
            pltpu.VMEM((2, 2, 4, T, T), f32),
            pltpu.VMEM((2, 2, 2, T, T), f32),
            pltpu.VMEM((2, 2, T, T), f32),
            pltpu.VMEM((n - 1, 8, T), f32),
            pltpu.VMEM((8, T), f32),
            *both(2, 2, 4), *both(2, 2, 2), *both(2, 2), *both(n - 1), *both(2, 2),
            *both(2, 2), *both(2, 2, 2), *both(2, 2, 4), dma(6), dma(tiles),
        ],
        compiler_params=pltpu.CompilerParams(collective_id=cid, has_side_effects=True, vmem_limit_bytes=24 << 20),
        name=f"share_{mask}",
    )(grads, counts, pin(block) if mask else block)


def local(user_factors, item_factors, ratings, user_tile, item_tile, live_count, partner):
    n = lax.axis_size("replica")
    half = lax.axis_size("stratum") // 2
    users, grads, counts = tiles_step(0, user_tile, item_tile, live_count, user_factors, item_factors, ratings, n)
    branches = [functools.partial(share, mask=half + k, cid=1 + k) for k in range(half)]
    block = lax.switch(partner[0] - half, branches, grads, counts, item_factors)
    users, grads, counts = tiles_step(1, user_tile, item_tile, live_count, users, block, ratings, n)
    return users, share(grads, counts, block, 0, 0)


def solution(mesh):
    return jax.shard_map(
        local,
        mesh=mesh,
        in_specs=(
            P(("stratum", "replica"), None),
            P("stratum", None),
            P(None, ("stratum", "replica"), None, None),
            P(None, ("stratum", "replica")),
            P(None, ("stratum", "replica")),
            P(None, ("stratum", "replica")),
            P(),
        ),
        out_specs=(P(("stratum", "replica"), None), P("stratum", None)),
        check_vma=False,
    )
```

```python
import functools

import jax
import jax.numpy as jnp
from jax import lax
from jax.experimental import pallas as pl
from jax.experimental.pallas import tpu as pltpu
from jax.sharding import PartitionSpec as P

LR = 0.05
KEEP = 1.0 - 0.05 * 0.05
NT = (((1,), (1,)), ((), ()))
NN = (((1,), (0,)), ((), ()))
f32, bf16, i32 = jnp.float32, jnp.bfloat16, jnp.int32
GROUP = 16


def pin(x, space=pltpu.HBM):
    return pltpu.with_memory_space_constraint(x, space)


def tile_kernel(epoch, shards, chunks, ut_in, it_in, live_in, users, items, ratings,
                users_out, dv, counts_out,
                ut, it, live_ref, rat, uf, vf, ub, utb, vb, du,
                rbuf, pa, p1, p2, nb, pend, su, si, rsem, msem, osem):
    tiles, T = ub.shape[0], ub.shape[1]
    slots = rat.shape[0]
    width = slots // chunks
    first = epoch == 0
    per = slots // tiles

    def load(c):
        o = pl.ds(c * width, width)
        return pltpu.make_async_copy(ratings.at[epoch, o], rat.at[o], rsem.at[c])

    def rows(b):
        return pl.ds(pl.multiple_of(b * T, T), T)

    small = [pltpu.make_async_copy(ut_in, ut, msem.at[0]), pltpu.make_async_copy(it_in, it, msem.at[1]),
             pltpu.make_async_copy(live_in, live_ref, msem.at[2])]
    big = [pltpu.make_async_copy(users, uf, msem.at[3]), pltpu.make_async_copy(items, vf, msem.at[4])]
    for cp in small + big:
        cp.start()
    for c in range(chunks):
        load(c).start()

    @pl.loop(0, tiles)
    def _(b):
        su[b] = 0
        si[b] = 0
        pend[b] = -1
        du[b] = jnp.zeros((T, T), f32)
        dv[b] = jnp.zeros((T, T), f32)

    for cp in small:
        cp.wait()
    live = live_ref[epoch]

    @functools.partial(lax.fori_loop, 0, tiles // 2, init_val=jnp.int32(GROUP))
    def pairs(i, np):
        for k in range(2 * per):
            t = i * (2 * per) + k
            a, b = ut[epoch, t], it[epoch, t]
            valid = t < live
            q = pend[a]
            has = jnp.logical_and(valid, q >= 0)
            pa[np] = a
            p1[np] = q
            p2[np] = t
            np = np + has.astype(i32)
            pend[a] = jnp.where(valid, jnp.where(has, -1, t), q)
            one = valid.astype(i32)
            su[a] = su[a] + one
            si[b] = si[b] + one
        nb[i] = np
        return np

    for cp in big:
        cp.wait()
    eye = (lax.broadcasted_iota(i32, (T, T), 0) == lax.broadcasted_iota(i32, (T, T), 1)).astype(bf16)

    @pl.loop(0, tiles // 4)
    def _(i):
        for k in range(4):
            b = i * 4 + k
            x = uf[rows(b), :].astype(bf16)
            ub[b] = x
            utb[b] = lax.dot_general(eye, x, NT, preferred_element_type=f32).astype(bf16)
            vb[b] = vf[rows(b), :].astype(bf16)

    @functools.partial(lax.fori_loop, 0, tiles, init_val=pairs)
    def total(a, np):
        q = pend[a]
        pa[np] = a
        p1[np] = q
        p2[np] = -1
        return np + (q >= 0).astype(i32)

    for k in range(GROUP):
        for o in (0, total):
            pa[o + k] = 0
            p1[o + k] = -1
            p2[o + k] = -1

    rbuf[...] = jnp.zeros(rbuf.shape, bf16)

    def names(g):
        out = []
        for k in range(GROUP):
            p = g * GROUP + k
            x, y = p1[p], p2[p]
            tx, ty = jnp.maximum(x, 0), jnp.maximum(y, 0)
            out.append((pa[p], x, y, tx, ty, it[epoch, tx], it[epoch, ty]))
        return out

    def flush(g):
        todo = names(g)
        gu, gv = [], []
        for k, (a, x, y, tx, ty, bx, by) in enumerate(todo):
            r = rbuf[k]
            v = jnp.concatenate([vb[bx], vb[by]], axis=0)
            gu.append(lax.dot_general(r, v, NN, preferred_element_type=f32))
            gv.append(lax.dot_general(utb[a], r, NN, preferred_element_type=f32))
        return todo, gu, gv

    def fill(g):
        res = []
        for k, (a, x, y, tx, ty, bx, by) in enumerate(names(g)):
            v = jnp.concatenate([vb[bx], vb[by]], axis=0)
            p = lax.dot_general(ub[a], v, NT, preferred_element_type=f32)
            r1 = (rat[tx].astype(f32) - p[:, :T]).astype(bf16)
            r2 = (rat[ty].astype(f32) - p[:, T:]).astype(bf16)
            zero = jnp.zeros((T, T), bf16)
            res.append(jnp.concatenate([jnp.where(x >= 0, r1, zero), jnp.where(y >= 0, r2, zero)], axis=1))
        return res

    def settle(todo, gu, gv):
        for k, (a, x, y, tx, ty, bx, by) in enumerate(todo):
            du[a] += gu[k]
            dv[bx] += gv[k][:, :T]
            dv[by] += gv[k][:, T:]

    def work(g, carry):
        todo, gu, gv = flush(g)
        res = fill(g + 1)
        for k in range(GROUP):
            rbuf[k] = res[k]
        settle(todo, gu, gv)
        return carry

    def chunk(c, done):
        load(c).wait()
        upto = nb[(c + 1) * (tiles // 2 // chunks) - 1] // GROUP - 1
        upto = jnp.where(c == chunks - 1, pl.cdiv(total, GROUP) - 1, upto)
        lax.fori_loop(done, upto, work, 0)
        return jnp.maximum(done, upto)

    ended = lax.fori_loop(0, chunks, chunk, jnp.int32(0))
    settle(*flush(ended))

    row = lax.broadcasted_iota(i32, (8, T), 0)
    for r in range(shards):
        x, hy = r // 2, r % 2
        lo, hi = x % 2, x // 2
        z = jnp.zeros((8, T), f32)
        for d in range(2):
            for c in range(2):
                b = (d * 2 + c) * 8 + (hi if d else lo ^ hi) * 4 + hy * 2 + lo
                z = jnp.where(row == d * 2 + c, si[b].astype(f32), z)
        counts_out[r] = z


    def update(i, carry):
        for k in range(2):
            b = i * 2 + k
            cnt = jnp.full((1, T), jnp.maximum(su[b], 1), i32).astype(f32)
            uf[rows(b), :] = uf[rows(b), :] * KEEP + du[b] * (LR / cnt)
        return carry

    quarter = tiles // 4
    sent = []
    for part in range(4):
        lax.fori_loop(part * quarter // 2, (part + 1) * quarter // 2, update, 0)
        o = pl.ds(part * quarter * T, quarter * T)
        sent.append(pltpu.make_async_copy(uf.at[o], users_out.at[o], osem.at[part]))
        sent[-1].start()
    for cp in sent:
        cp.wait()


def tiles_step(epoch, ut, it, live, users, items, ratings, shards=8, chunks=8):
    slots, T = ratings.shape[1], ratings.shape[2]
    tiles = users.shape[0] // T
    first = epoch == 0
    hbm = pl.BlockSpec(memory_space=pltpu.HBM)
    vmem = pl.BlockSpec(memory_space=pltpu.VMEM)
    smem = lambda *k: pltpu.SMEM(k, i32)
    length = slots // 2 + tiles + 2 * GROUP
    return pl.pallas_call(
        functools.partial(tile_kernel, epoch, shards, chunks),
        out_shape=(pltpu.HBM(users.shape, f32), pltpu.VMEM((tiles, T, T), f32), pltpu.VMEM((shards, 8, T), f32)),
        in_specs=[hbm] * 4 + [hbm if first else pl.BlockSpec(memory_space=pl.ANY)] + [hbm],
        out_specs=(hbm, vmem, vmem),
        scratch_shapes=[
            smem(*ut.shape), smem(*it.shape), smem(*live.shape),
            pltpu.VMEM((slots, T, T), bf16),
            pltpu.VMEM(users.shape, f32),
            pltpu.VMEM(items.shape, f32),
            pltpu.VMEM((tiles, T, T), bf16), pltpu.VMEM((tiles, T, T), bf16), pltpu.VMEM((tiles, T, T), bf16),
            pltpu.VMEM((tiles, T, T), f32),
            pltpu.VMEM((GROUP, T, 2 * T), bf16),
            smem(length), smem(length), smem(length), smem(tiles // 2), smem(tiles), smem(tiles), smem(tiles),
            pltpu.SemaphoreType.DMA((chunks,)), pltpu.SemaphoreType.DMA((5,)), pltpu.SemaphoreType.DMA((4,)),
        ],
        compiler_params=pltpu.CompilerParams(vmem_limit_bytes=32 << 20),
        name=f"tile_step_{epoch}",
    )(pin(ut), pin(it), pin(live), pin(users), pin(items) if first else items, pin(ratings))


MESH = pl.DeviceIdType.MESH


def share_kernel(mask, grads, counts, block, dest, hold, acc, old, new, rx1, ry, rx2, cin, cmine,
                 s1, r1, sy, ry_s, s2, r2, sc, rc, se, re, t2, q2, ty, qy, t1, q1, lsem, wsem):
    T = block.shape[1]
    n = counts.shape[0]
    s = lax.axis_index("stratum")
    r = lax.axis_index("replica")
    x, hy = lax.div(r, 2), lax.rem(r, 2)
    lo, hi = lax.rem(x, 2), lax.div(x, 2)
    xa = x + 1 - 2 * lo
    xb = 3 - x
    at = lambda x_, y_: (s, x_ * 2 + y_)
    first = (at(xa, hy), at(xb, hy))
    second = (at(xb, hy), at(xa, hy))
    over = at(x, 1 - hy)
    h1 = (lo + hi - 2 * lo * hi, hi)
    h2 = (lo, lo)

    def tile(d, c, a, b, e):
        return (d * 2 + c) * 8 + a * 4 + b * 2 + e

    def put(src, dst, ss, rs, dev):
        cp = pltpu.make_async_remote_copy(src_ref=src, dst_ref=dst, send_sem=ss, recv_sem=rs, device_id=dev, device_id_type=MESH)
        cp.start()
        return cp

    def rows(b):
        return pl.ds(pl.multiple_of(b * T, T), T)

    out = hold if mask else dest
    saved = []

    def save(b):
        if mask:
            saved.append(pltpu.make_async_copy(out.at[rows(b)], dest.at[rows(b)], wsem.at[len(saved)]))
            saved[-1].start()

    bar = pltpu.get_barrier_semaphore()
    for k in range(1, n):
        pl.semaphore_signal(bar, inc=1, device_id=(s, lax.rem(r + k, n)), device_id_type=MESH)
    across = s
    if mask:
        for bit in range(4):
            if mask >> bit & 1:
                across = across + (1 << bit) - (2 << bit) * lax.rem(lax.div(s, 1 << bit), 2)
        pl.semaphore_signal(bar, inc=1, device_id=(across, r), device_id_type=MESH)
    local = [pltpu.make_async_copy(counts.at[r], cmine, lsem.at[1])]
    mine = {}
    for d in range(2):
        for c in range(2):
            b = tile(d, c, h1[d], hy, h2[d])
            mine[d, c] = b
            local.append(pltpu.make_async_copy(block.at[rows(b)], old.at[d, c], lsem.at[2 + d * 2 + c]))
    for cp in local:
        cp.start()
    pl.semaphore_wait(bar, n - 1 + (1 if mask else 0))

    pend = []
    got1, goty, got2, gote = {}, {}, {}, {}
    for c in range(2):
        for half in range(2):
            for e in range(2):
                for d in range(2):
                    i = half * 2 + e
                    yb = hy if half else 1 - hy
                    eb = 1 - h2[d] if e else h2[d]
                    got1[d, c, i] = put(grads.at[tile(d, c, 1 - h1[d], yb, eb)], rx1.at[d, c, i], s1.at[d, c, i], r1.at[d, c, i], first[d])
        if not c:
            gotc = [put(counts.at[lax.rem(r + k, n)], cin.at[k - 1], sc.at[k - 1], rc.at[k - 1], (s, lax.rem(r + k, n))) for k in range(1, n)]
    for cp in local:
        cp.wait()

    def add(d, c, a, b, e, part):
        t = tile(d, c, a, b, e)
        acc[t] = acc[t] + part[...]

    def take1(c, i):
        for d in range(2):
            e = h2[d] if i % 2 else 1 - h2[d]
            b = hy if i >= 2 else 1 - hy
            got1[d, c, i].wait_recv()
            t = tile(d, c, h1[d], b, e)
            acc[t] = grads[t] + rx1[d, c, i]
            if i < 2:
                goty[d, c, i] = put(acc.at[tile(d, c, h1[d], b, e)], ry.at[d, c, i], sy.at[d, c, i], ry_s.at[d, c, i], over)

    def takey(c, j):
        for d in range(2):
            e = h2[d] if j else 1 - h2[d]
            goty[d, c, j].wait_recv()
            add(d, c, h1[d], hy, e, ry.at[d, c, j])
            if j == 0:
                got2[d, c] = put(acc.at[tile(d, c, h1[d], hy, e)], rx2.at[d, c], s2.at[d, c], r2.at[d, c], second[d])

    own = {}
    def finish(c):
        for d in range(2):
            b = mine[d, c]
            got2[d, c].wait_recv()
            total = acc[b] + rx2[d, c]
            cnt = jnp.maximum(cmine[pl.ds(d * 2 + c, 1), :], 1.0)
            fresh = old[d, c] * KEEP + total.T * (LR / cnt)
            if mask:
                new[d, c] = fresh
                gote[d, c] = put(new.at[d, c], out.at[rows(b)], se.at[d, c], re.at[d, c], (across, r))
            else:
                out[rows(b), :] = fresh

    ag2, agy, ag1 = {}, {}, {}

    def send2(d, c, b):
        ag2[d, c] = put(out.at[rows(b)], out.at[rows(b)], t2.at[d, c], q2.at[d, c], second[d])

    def sendy(d, c, j, b):
        agy[d, c, j] = put(out.at[rows(b)], out.at[rows(b)], ty.at[d, c, j], qy.at[d, c, j], over)

    def send1(d, c, i, b):
        ag1[d, c, i] = put(out.at[rows(b)], out.at[rows(b)], t1.at[d, c, i], q1.at[d, c, i], first[d])

    def spread(c):
        for d in range(2):
            b = mine[d, c]
            if mask:
                gote[d, c].wait_recv()
            send2(d, c, b)
            sendy(d, c, 0, b)
            send1(d, c, 0, b)
            save(b)

    def pass2(c):
        for d in range(2):
            ag2[d, c].wait_recv()
            b = tile(d, c, h1[d], hy, 1 - h2[d])
            sendy(d, c, 1, b)
            send1(d, c, 1, b)
            save(b)

    def passy(c, j):
        for d in range(2):
            agy[d, c, j].wait_recv()
            b = tile(d, c, h1[d], 1 - hy, 1 - h2[d] if j else h2[d])
            send1(d, c, 2 + j, b)
            save(b)

    take1(0, 0)
    take1(0, 1)
    take1(0, 2)
    takey(0, 0)
    take1(0, 3)
    for g in gotc:
        g.wait_recv()
    cmine[...] += functools.reduce(lambda p, q: p + q, [cin[k] for k in range(n - 1)])
    takey(0, 1)
    take1(1, 0)
    finish(0)
    take1(1, 1)
    take1(1, 2)
    takey(1, 0)
    take1(1, 3)
    spread(0)
    takey(1, 1)
    finish(1)
    pass2(0)
    passy(0, 0)
    passy(0, 1)
    spread(1)
    pass2(1)
    passy(1, 0)
    passy(1, 1)
    for c in range(2):
        for i in range(4):
            for d in range(2):
                ag1[d, c, i].wait_recv()
                save(tile(d, c, 1 - h1[d], 1 - hy if i >= 2 else hy, h2[d] if i % 2 else 1 - h2[d]))
    for table in (got1, goty, got2, gote, ag2, agy, ag1):
        for cp in table.values():
            cp.wait_send()
    for g in gotc:
        g.wait_send()
    for cp in saved:
        cp.wait()


def share(grads, counts, block, mask, cid):
    tiles, T = grads.shape[0], grads.shape[1]
    n = counts.shape[0]
    vmem = pl.BlockSpec(memory_space=pltpu.VMEM)
    hbm = pl.BlockSpec(memory_space=pltpu.HBM)
    dma = lambda *k: pltpu.SemaphoreType.DMA(k)
    both = lambda *k: [dma(*k), dma(*k)]
    return pl.pallas_call(
        functools.partial(share_kernel, mask),
        out_shape=(pltpu.HBM if mask else pltpu.VMEM)(block.shape, f32),
        in_specs=[vmem, vmem, hbm if mask else pl.BlockSpec(memory_space=pl.ANY)],
        out_specs=hbm if mask else vmem,
        scratch_shapes=[
            pltpu.VMEM(block.shape if mask else (8, T), f32),
            pltpu.VMEM((tiles, T, T), f32),
            pltpu.VMEM((2, 2, T, T), f32),
            pltpu.VMEM((2, 2, T, T), f32),
            pltpu.VMEM((2, 2, 4, T, T), f32),
            pltpu.VMEM((2, 2, 2, T, T), f32),
            pltpu.VMEM((2, 2, T, T), f32),
            pltpu.VMEM((n - 1, 8, T), f32),
            pltpu.VMEM((8, T), f32),
            *both(2, 2, 4), *both(2, 2, 2), *both(2, 2), *both(n - 1), *both(2, 2),
            *both(2, 2), *both(2, 2, 2), *both(2, 2, 4), dma(6), dma(tiles),
        ],
        compiler_params=pltpu.CompilerParams(collective_id=cid, has_side_effects=True, vmem_limit_bytes=24 << 20),
        name=f"share_{mask}",
    )(grads, counts, pin(block) if mask else block)


def local(user_factors, item_factors, ratings, user_tile, item_tile, live_count, partner):
    n = lax.axis_size("replica")
    half = lax.axis_size("stratum") // 2
    live_count = live_count.reshape(-1)
    users, grads, counts = tiles_step(0, user_tile, item_tile, live_count, user_factors, item_factors, ratings, n)
    branches = [functools.partial(share, mask=half + k, cid=1 + k) for k in range(half)]
    block = lax.switch(partner[0] - half, branches, grads, counts, item_factors)
    users, grads, counts = tiles_step(1, user_tile, item_tile, live_count, users, block, ratings, n)
    return users, share(grads, counts, block, 0, 0)


def solution(mesh):
    return jax.shard_map(
        local,
        mesh=mesh,
        in_specs=(
            P(("stratum", "replica"), None),
            P("stratum", None),
            P(None, ("stratum", "replica"), None, None),
            P(None, ("stratum", "replica")),
            P(None, ("stratum", "replica")),
            P(None, ("stratum", "replica")),
            P(),
        ),
        out_specs=(P(("stratum", "replica"), None), P("stratum", None)),
        check_vma=False,
    )
```

```python
import functools

import jax
import jax.numpy as jnp
from jax import lax
from jax.experimental import pallas as pl
from jax.experimental.pallas import tpu as pltpu
from jax.sharding import PartitionSpec as P

LR = 0.05
KEEP = 1.0 - 0.05 * 0.05
NT = (((1,), (1,)), ((), ()))
NN = (((1,), (0,)), ((), ()))
f32, bf16, i32 = jnp.float32, jnp.bfloat16, jnp.int32
GROUP = 16


def pin(x, space=pltpu.HBM):
    return pltpu.with_memory_space_constraint(x, space)


def tile_kernel(epoch, shards, chunks, ut_in, it_in, live_in, users, items, ratings,
                users_out, dv, counts_out,
                ut, it, live_ref, rat, uf, vf, ub, utb, vb, du,
                rbuf, pa, p1, p2, nb, pend, su, si, rsem, msem, osem):
    tiles, T = ub.shape[0], ub.shape[1]
    slots = rat.shape[0]
    width = slots // chunks
    first = epoch == 0
    per = slots // tiles

    def load(c):
        o = pl.ds(c * width, width)
        return pltpu.make_async_copy(ratings.at[epoch, o], rat.at[o], rsem.at[c])

    def rows(b):
        return pl.ds(pl.multiple_of(b * T, T), T)

    small = [pltpu.make_async_copy(ut_in, ut, msem.at[0]), pltpu.make_async_copy(it_in, it, msem.at[1]),
             pltpu.make_async_copy(live_in, live_ref, msem.at[2])]
    big = [pltpu.make_async_copy(users, uf, msem.at[3]), pltpu.make_async_copy(items, vf, msem.at[4])]
    for cp in small + big:
        cp.start()
    for c in range(2):
        load(c).start()

    @pl.loop(0, tiles)
    def _(b):
        su[b] = 0
        si[b] = 0
        pend[b] = -1
        du[b] = jnp.zeros((T, T), f32)
        dv[b] = jnp.zeros((T, T), f32)

    for cp in small:
        cp.wait()
    live = live_ref[epoch]

    @functools.partial(lax.fori_loop, 0, tiles // 2, init_val=jnp.int32(GROUP))
    def pairs(i, np):
        for k in range(2 * per):
            t = i * (2 * per) + k
            a, b = ut[epoch, t], it[epoch, t]
            valid = t < live
            q = pend[a]
            has = jnp.logical_and(valid, q >= 0)
            pa[np] = a
            p1[np] = q
            p2[np] = t
            np = np + has.astype(i32)
            pend[a] = jnp.where(valid, jnp.where(has, -1, t), q)
            one = valid.astype(i32)
            su[a] = su[a] + one
            si[b] = si[b] + one
        nb[i] = np
        return np

    for c in range(2, chunks):
        load(c).start()
    for cp in big:
        cp.wait()
    eye = (lax.broadcasted_iota(i32, (T, T), 0) == lax.broadcasted_iota(i32, (T, T), 1)).astype(bf16)

    @pl.loop(0, tiles // 4)
    def _(i):
        for k in range(4):
            b = i * 4 + k
            x = uf[rows(b), :].astype(bf16)
            ub[b] = x
            utb[b] = lax.dot_general(eye, x, NT, preferred_element_type=f32).astype(bf16)
            vb[b] = vf[rows(b), :].astype(bf16)

    @functools.partial(lax.fori_loop, 0, tiles, init_val=pairs)
    def total(a, np):
        q = pend[a]
        pa[np] = a
        p1[np] = q
        p2[np] = -1
        return np + (q >= 0).astype(i32)

    for k in range(GROUP):
        for o in (0, total):
            pa[o + k] = 0
            p1[o + k] = -1
            p2[o + k] = -1

    rbuf[...] = jnp.zeros(rbuf.shape, bf16)

    def names(g):
        out = []
        for k in range(GROUP):
            p = g * GROUP + k
            x, y = p1[p], p2[p]
            tx, ty = jnp.maximum(x, 0), jnp.maximum(y, 0)
            out.append((pa[p], x, y, tx, ty, it[epoch, tx], it[epoch, ty]))
        return out

    def flush(k, name):
        a, x, y, tx, ty, bx, by = name
        r = rbuf[k]
        v = jnp.concatenate([vb[bx], vb[by]], axis=0)
        gu = lax.dot_general(r, v, NN, preferred_element_type=f32)
        gv = lax.dot_general(utb[a], r, NN, preferred_element_type=f32)
        return gu, gv

    def settle(name, gu, gv):
        a, x, y, tx, ty, bx, by = name
        du[a] += gu
        dv[bx] += gv[:, :T]
        dv[by] += gv[:, T:]

    def fill(k, name):
        a, x, y, tx, ty, bx, by = name
        v = jnp.concatenate([vb[bx], vb[by]], axis=0)
        p = lax.dot_general(ub[a], v, NT, preferred_element_type=f32)
        r1 = (rat[tx].astype(f32) - p[:, :T]).astype(bf16)
        r2 = (rat[ty].astype(f32) - p[:, T:]).astype(bf16)
        zero = jnp.zeros((T, T), bf16)
        rbuf[k] = jnp.concatenate([jnp.where(x >= 0, r1, zero), jnp.where(y >= 0, r2, zero)], axis=1)

    def work(g, carry):
        now, later = names(g), names(g + 1)
        for k in range(GROUP):
            gu, gv = flush(k, now[k])
            fill(k, later[k])
            settle(now[k], gu, gv)
        return carry

    def chunk(c, done):
        load(c).wait()
        upto = nb[(c + 1) * (tiles // 2 // chunks) - 1] // GROUP - 1
        upto = jnp.where(c == chunks - 1, pl.cdiv(total, GROUP) - 1, upto)
        lax.fori_loop(done, upto, work, 0)
        return jnp.maximum(done, upto)

    ended = lax.fori_loop(0, chunks, chunk, jnp.int32(0))
    last = names(ended)
    for k in range(GROUP):
        settle(last[k], *flush(k, last[k]))

    row = lax.broadcasted_iota(i32, (8, T), 0)
    for r in range(shards):
        x, hy = r // 2, r % 2
        lo, hi = x % 2, x // 2
        z = jnp.zeros((8, T), f32)
        for d in range(2):
            for c in range(2):
                b = (d * 2 + c) * 8 + (hi if d else lo ^ hi) * 4 + hy * 2 + lo
                z = jnp.where(row == d * 2 + c, si[b].astype(f32), z)
        counts_out[r] = z


    def update(i, carry):
        for k in range(2):
            b = i * 2 + k
            cnt = jnp.full((1, T), jnp.maximum(su[b], 1), i32).astype(f32)
            uf[rows(b), :] = uf[rows(b), :] * KEEP + du[b] * (LR / cnt)
        return carry

    quarter = tiles // 4
    sent = []
    for part in range(4):
        lax.fori_loop(part * quarter // 2, (part + 1) * quarter // 2, update, 0)
        o = pl.ds(part * quarter * T, quarter * T)
        sent.append(pltpu.make_async_copy(uf.at[o], users_out.at[o], osem.at[part]))
        sent[-1].start()
    for cp in sent:
        cp.wait()


def tiles_step(epoch, ut, it, live, users, items, ratings, shards=8, chunks=8):
    slots, T = ratings.shape[1], ratings.shape[2]
    tiles = users.shape[0] // T
    first = epoch == 0
    hbm = pl.BlockSpec(memory_space=pltpu.HBM)
    vmem = pl.BlockSpec(memory_space=pltpu.VMEM)
    smem = lambda *k: pltpu.SMEM(k, i32)
    length = slots // 2 + tiles + 2 * GROUP
    return pl.pallas_call(
        functools.partial(tile_kernel, epoch, shards, chunks),
        out_shape=(pltpu.HBM(users.shape, f32), pltpu.VMEM((tiles, T, T), f32), pltpu.VMEM((shards, 8, T), f32)),
        in_specs=[hbm] * 4 + [hbm if first else pl.BlockSpec(memory_space=pl.ANY)] + [hbm],
        out_specs=(hbm, vmem, vmem),
        scratch_shapes=[
            smem(*ut.shape), smem(*it.shape), smem(*live.shape),
            pltpu.VMEM((slots, T, T), bf16),
            pltpu.VMEM(users.shape, f32),
            pltpu.VMEM(items.shape, f32),
            pltpu.VMEM((tiles, T, T), bf16), pltpu.VMEM((tiles, T, T), bf16), pltpu.VMEM((tiles, T, T), bf16),
            pltpu.VMEM((tiles, T, T), f32),
            pltpu.VMEM((GROUP, T, 2 * T), bf16),
            smem(length), smem(length), smem(length), smem(tiles // 2), smem(tiles), smem(tiles), smem(tiles),
            pltpu.SemaphoreType.DMA((chunks,)), pltpu.SemaphoreType.DMA((5,)), pltpu.SemaphoreType.DMA((4,)),
        ],
        compiler_params=pltpu.CompilerParams(vmem_limit_bytes=32 << 20),
        name=f"tile_step_{epoch}",
    )(pin(ut), pin(it), pin(live), pin(users), pin(items) if first else items, pin(ratings))


MESH = pl.DeviceIdType.MESH


def share_kernel(mask, grads, counts, block, dest, hold, acc, old, new, rx1, ry, rx2, cin, cmine,
                 s1, r1, sy, ry_s, s2, r2, sc, rc, se, re, t2, q2, ty, qy, t1, q1, lsem, wsem):
    T = block.shape[1]
    n = counts.shape[0]
    s = lax.axis_index("stratum")
    r = lax.axis_index("replica")
    x, hy = lax.div(r, 2), lax.rem(r, 2)
    lo, hi = lax.rem(x, 2), lax.div(x, 2)
    xa = x + 1 - 2 * lo
    xb = 3 - x
    at = lambda x_, y_: (s, x_ * 2 + y_)
    first = (at(xa, hy), at(xb, hy))
    second = (at(xb, hy), at(xa, hy))
    over = at(x, 1 - hy)
    h1 = (lo + hi - 2 * lo * hi, hi)
    h2 = (lo, lo)

    def tile(d, c, a, b, e):
        return (d * 2 + c) * 8 + a * 4 + b * 2 + e

    def put(src, dst, ss, rs, dev):
        cp = pltpu.make_async_remote_copy(src_ref=src, dst_ref=dst, send_sem=ss, recv_sem=rs, device_id=dev, device_id_type=MESH)
        cp.start()
        return cp

    def rows(b):
        return pl.ds(pl.multiple_of(b * T, T), T)

    out = hold if mask else dest
    saved = []

    def save(b):
        if mask:
            saved.append(pltpu.make_async_copy(out.at[rows(b)], dest.at[rows(b)], wsem.at[len(saved)]))
            saved[-1].start()

    bar = pltpu.get_barrier_semaphore()
    for k in range(1, n):
        pl.semaphore_signal(bar, inc=1, device_id=(s, lax.rem(r + k, n)), device_id_type=MESH)
    across = s
    if mask:
        for bit in range(4):
            if mask >> bit & 1:
                across = across + (1 << bit) - (2 << bit) * lax.rem(lax.div(s, 1 << bit), 2)
        pl.semaphore_signal(bar, inc=1, device_id=(across, r), device_id_type=MESH)
    local = [pltpu.make_async_copy(counts.at[r], cmine, lsem.at[1])]
    mine = {}
    for d in range(2):
        for c in range(2):
            b = tile(d, c, h1[d], hy, h2[d])
            mine[d, c] = b
            local.append(pltpu.make_async_copy(block.at[rows(b)], old.at[d, c], lsem.at[2 + d * 2 + c]))
    for cp in local:
        cp.start()
    pl.semaphore_wait(bar, n - 1 + (1 if mask else 0))

    pend = []
    got1, goty, got2, gote = {}, {}, {}, {}
    def go(c, half):
        for e in range(2):
            for d in range(2):
                i = half * 2 + e
                yb = hy if half else 1 - hy
                eb = 1 - h2[d] if e else h2[d]
                got1[d, c, i] = put(grads.at[tile(d, c, 1 - h1[d], yb, eb)], rx1.at[d, c, i], s1.at[d, c, i], r1.at[d, c, i], first[d])

    go(0, 0)
    go(0, 1)
    gotc = [put(counts.at[lax.rem(r + k, n)], cin.at[k - 1], sc.at[k - 1], rc.at[k - 1], (s, lax.rem(r + k, n))) for k in range(1, n)]
    for cp in local:
        cp.wait()

    def add(d, c, a, b, e, part):
        t = tile(d, c, a, b, e)
        acc[t] = acc[t] + part[...]

    def take1(c, i):
        for d in range(2):
            e = h2[d] if i % 2 else 1 - h2[d]
            b = hy if i >= 2 else 1 - hy
            got1[d, c, i].wait_recv()
            t = tile(d, c, h1[d], b, e)
            acc[t] = grads[t] + rx1[d, c, i]
            if i < 2:
                goty[d, c, i] = put(acc.at[tile(d, c, h1[d], b, e)], ry.at[d, c, i], sy.at[d, c, i], ry_s.at[d, c, i], over)

    def takey(c, j):
        for d in range(2):
            e = h2[d] if j else 1 - h2[d]
            goty[d, c, j].wait_recv()
            add(d, c, h1[d], hy, e, ry.at[d, c, j])
            if j == 0:
                got2[d, c] = put(acc.at[tile(d, c, h1[d], hy, e)], rx2.at[d, c], s2.at[d, c], r2.at[d, c], second[d])

    own = {}
    def finish(c):
        for d in range(2):
            b = mine[d, c]
            got2[d, c].wait_recv()
            total = acc[b] + rx2[d, c]
            cnt = jnp.maximum(cmine[pl.ds(d * 2 + c, 1), :], 1.0)
            fresh = old[d, c] * KEEP + total.T * (LR / cnt)
            if mask:
                new[d, c] = fresh
                gote[d, c] = put(new.at[d, c], out.at[rows(b)], se.at[d, c], re.at[d, c], (across, r))
            else:
                out[rows(b), :] = fresh

    ag2, agy, ag1 = {}, {}, {}

    def send2(d, c, b):
        ag2[d, c] = put(out.at[rows(b)], out.at[rows(b)], t2.at[d, c], q2.at[d, c], second[d])

    def sendy(d, c, j, b):
        agy[d, c, j] = put(out.at[rows(b)], out.at[rows(b)], ty.at[d, c, j], qy.at[d, c, j], over)

    def send1(d, c, i, b):
        ag1[d, c, i] = put(out.at[rows(b)], out.at[rows(b)], t1.at[d, c, i], q1.at[d, c, i], first[d])

    def spread(c):
        for d in range(2):
            b = mine[d, c]
            if mask:
                gote[d, c].wait_recv()
            send2(d, c, b)
            sendy(d, c, 0, b)
            send1(d, c, 0, b)
            save(b)

    def pass2(c):
        for d in range(2):
            ag2[d, c].wait_recv()
            b = tile(d, c, h1[d], hy, 1 - h2[d])
            sendy(d, c, 1, b)
            send1(d, c, 1, b)
            save(b)

    def passy(c, j):
        for d in range(2):
            agy[d, c, j].wait_recv()
            b = tile(d, c, h1[d], 1 - hy, 1 - h2[d] if j else h2[d])
            send1(d, c, 2 + j, b)
            save(b)

    take1(0, 0)
    take1(0, 1)
    go(1, 0)
    take1(0, 2)
    take1(0, 3)
    for g in gotc:
        g.wait_recv()
    cmine[...] += functools.reduce(lambda p, q: p + q, [cin[k] for k in range(n - 1)])
    takey(0, 0)
    go(1, 1)
    take1(1, 0)
    take1(1, 1)
    takey(0, 1)
    finish(0)
    if not mask:
        spread(0)
    take1(1, 2)
    takey(1, 0)
    take1(1, 3)
    if not mask:
        pass2(0)
    takey(1, 1)
    finish(1)
    if mask:
        spread(0)
    if mask:
        pass2(0)
    spread(1)
    passy(0, 0)
    pass2(1)
    passy(0, 1)
    passy(1, 0)
    passy(1, 1)
    for c in range(2):
        for i in range(4):
            for d in range(2):
                ag1[d, c, i].wait_recv()
                save(tile(d, c, 1 - h1[d], 1 - hy if i >= 2 else hy, h2[d] if i % 2 else 1 - h2[d]))
    for table in (got1, goty, got2, gote, ag2, agy, ag1):
        for cp in table.values():
            cp.wait_send()
    for g in gotc:
        g.wait_send()
    for cp in saved:
        cp.wait()


def share(grads, counts, block, mask, cid):
    tiles, T = grads.shape[0], grads.shape[1]
    n = counts.shape[0]
    vmem = pl.BlockSpec(memory_space=pltpu.VMEM)
    hbm = pl.BlockSpec(memory_space=pltpu.HBM)
    dma = lambda *k: pltpu.SemaphoreType.DMA(k)
    both = lambda *k: [dma(*k), dma(*k)]
    return pl.pallas_call(
        functools.partial(share_kernel, mask),
        out_shape=(pltpu.HBM if mask else pltpu.VMEM)(block.shape, f32),
        in_specs=[vmem, vmem, hbm if mask else pl.BlockSpec(memory_space=pl.ANY)],
        out_specs=hbm if mask else vmem,
        scratch_shapes=[
            pltpu.VMEM(block.shape if mask else (8, T), f32),
            pltpu.VMEM((tiles, T, T), f32),
            pltpu.VMEM((2, 2, T, T), f32),
            pltpu.VMEM((2, 2, T, T), f32),
            pltpu.VMEM((2, 2, 4, T, T), f32),
            pltpu.VMEM((2, 2, 2, T, T), f32),
            pltpu.VMEM((2, 2, T, T), f32),
            pltpu.VMEM((n - 1, 8, T), f32),
            pltpu.VMEM((8, T), f32),
            *both(2, 2, 4), *both(2, 2, 2), *both(2, 2), *both(n - 1), *both(2, 2),
            *both(2, 2), *both(2, 2, 2), *both(2, 2, 4), dma(6), dma(tiles),
        ],
        compiler_params=pltpu.CompilerParams(collective_id=cid, has_side_effects=True, vmem_limit_bytes=24 << 20),
        name=f"share_{mask}",
    )(grads, counts, pin(block) if mask else block)


def local(user_factors, item_factors, ratings, user_tile, item_tile, live_count, partner):
    n = lax.axis_size("replica")
    half = lax.axis_size("stratum") // 2
    live_count = live_count.reshape(-1)
    users, grads, counts = tiles_step(0, user_tile, item_tile, live_count, user_factors, item_factors, ratings, n)
    branches = [functools.partial(share, mask=half + k, cid=1 + k) for k in range(half)]
    block = lax.switch(partner[0] - half, branches, grads, counts, item_factors)
    users, grads, counts = tiles_step(1, user_tile, item_tile, live_count, users, block, ratings, n)
    return users, share(grads, counts, block, 0, 0)


def solution(mesh):
    return jax.shard_map(
        local,
        mesh=mesh,
        in_specs=(
            P(("stratum", "replica"), None),
            P("stratum", None),
            P(None, ("stratum", "replica"), None, None),
            P(None, ("stratum", "replica")),
            P(None, ("stratum", "replica")),
            P(None, ("stratum", "replica")),
            P(),
        ),
        out_specs=(P(("stratum", "replica"), None), P("stratum", None)),
        check_vma=False,
    )
```

```python
import functools

import jax
import jax.numpy as jnp
from jax import lax
from jax.experimental import pallas as pl
from jax.experimental.pallas import tpu as pltpu
from jax.sharding import PartitionSpec as P

LR = 0.05
KEEP = 1.0 - 0.05 * 0.05
NT = (((1,), (1,)), ((), ()))
NN = (((1,), (0,)), ((), ()))
f32, bf16, i32 = jnp.float32, jnp.bfloat16, jnp.int32
GROUP = 16


def pin(x, space=pltpu.HBM):
    return pltpu.with_memory_space_constraint(x, space)


def tile_kernel(epoch, chunks, ut_in, it_in, live_in, users, items, ratings,
                users_out, dv, counts_out,
                ut, it, live_ref, rat, uf, vf, ub, utb, vb, du,
                rbuf, pa, p1, p2, nb, pend, su, si, rsem, msem, osem):
    tiles, T = ub.shape[0], ub.shape[1]
    slots = rat.shape[0]
    width = slots // chunks
    first = epoch == 0
    per = slots // tiles

    def load(c):
        o = pl.ds(c * width, width)
        return pltpu.make_async_copy(ratings.at[epoch, o], rat.at[o], rsem.at[c])

    def rows(b):
        return pl.ds(pl.multiple_of(b * T, T), T)

    small = [pltpu.make_async_copy(ut_in, ut, msem.at[0]), pltpu.make_async_copy(it_in, it, msem.at[1]),
             pltpu.make_async_copy(live_in, live_ref, msem.at[2])]
    big = [pltpu.make_async_copy(users, uf, msem.at[3]), pltpu.make_async_copy(items, vf, msem.at[4])]
    for cp in small + big:
        cp.start()
    for c in range(2):
        load(c).start()

    @pl.loop(0, tiles)
    def _(b):
        su[b] = 0
        si[b] = 0
        pend[b] = -1
        du[b] = jnp.zeros((T, T), f32)
        dv[b] = jnp.zeros((T, T), f32)

    for cp in small:
        cp.wait()
    live = live_ref[epoch]

    def pair(i, np):
        for k in range(2 * per):
            t = i * (2 * per) + k
            a, b = ut[epoch, t], it[epoch, t]
            valid = t < live
            q = pend[a]
            has = jnp.logical_and(valid, q >= 0)
            pa[np] = a
            p1[np] = q
            p2[np] = t
            np = np + has.astype(i32)
            pend[a] = jnp.where(valid, jnp.where(has, -1, t), q)
            one = valid.astype(i32)
            su[a] = su[a] + one
            si[b] = si[b] + one
        nb[i] = np
        return np

    early = tiles // 4
    pairs = lax.fori_loop(0, early, pair, jnp.int32(GROUP))
    for c in range(2, chunks):
        load(c).start()
    for cp in big:
        cp.wait()
    eye = (lax.broadcasted_iota(i32, (T, T), 0) == lax.broadcasted_iota(i32, (T, T), 1)).astype(bf16)

    def cast(i, np):
        for k in range(4):
            b = i * 4 + k
            x = uf[rows(b), :].astype(bf16)
            ub[b] = x
            utb[b] = lax.dot_general(eye, x, NT, preferred_element_type=f32).astype(bf16)
            vb[b] = vf[rows(b), :].astype(bf16)
        return pair(early + i, np)

    pairs = lax.fori_loop(0, tiles // 4, cast, pairs)

    @functools.partial(lax.fori_loop, 0, tiles, init_val=pairs)
    def total(a, np):
        q = pend[a]
        pa[np] = a
        p1[np] = q
        p2[np] = -1
        return np + (q >= 0).astype(i32)

    for k in range(GROUP):
        for o in (0, total):
            pa[o + k] = 0
            p1[o + k] = -1
            p2[o + k] = -1

    rbuf[...] = jnp.zeros(rbuf.shape, bf16)

    def names(g):
        out = []
        for k in range(GROUP):
            p = g * GROUP + k
            x, y = p1[p], p2[p]
            tx, ty = jnp.maximum(x, 0), jnp.maximum(y, 0)
            out.append((pa[p], x, y, tx, ty, it[epoch, tx], it[epoch, ty]))
        return out

    def flush(k, name):
        a, x, y, tx, ty, bx, by = name
        r = rbuf[k]
        v = jnp.concatenate([vb[bx], vb[by]], axis=0)
        gu = lax.dot_general(r, v, NN, preferred_element_type=f32)
        gv = lax.dot_general(utb[a], r, NN, preferred_element_type=f32)
        return gu, gv

    def settle(name, gu, gv):
        a, x, y, tx, ty, bx, by = name
        du[a] += gu
        dv[bx] += gv[:, :T]
        dv[by] += gv[:, T:]

    def fill(k, name):
        a, x, y, tx, ty, bx, by = name
        v = jnp.concatenate([vb[bx], vb[by]], axis=0)
        p = lax.dot_general(ub[a], v, NT, preferred_element_type=f32)
        r1 = (rat[tx].astype(f32) - p[:, :T]).astype(bf16)
        r2 = (rat[ty].astype(f32) - p[:, T:]).astype(bf16)
        zero = jnp.zeros((T, T), bf16)
        rbuf[k] = jnp.concatenate([jnp.where(x >= 0, r1, zero), jnp.where(y >= 0, r2, zero)], axis=1)

    def work(g, carry):
        now, later = names(g), names(g + 1)
        for k in range(GROUP):
            gu, gv = flush(k, now[k])
            fill(k, later[k])
            settle(now[k], gu, gv)
        return carry

    def chunk(c, done):
        load(c).wait()
        upto = nb[(c + 1) * (tiles // 2 // chunks) - 1] // GROUP - 1
        upto = jnp.where(c == chunks - 1, pl.cdiv(total, GROUP) - 1, upto)
        lax.fori_loop(done, upto, work, 0)
        return jnp.maximum(done, upto)

    ended = lax.fori_loop(0, chunks, chunk, jnp.int32(0))
    last = names(ended)
    for k in range(GROUP):
        settle(last[k], *flush(k, last[k]))

    row = lax.broadcasted_iota(i32, (8, T), 0)
    for h in range(4):
        z = jnp.zeros((8, T), f32)
        for j in range(8):
            z = jnp.where(row == j, si[(h // 2 * 2 + j // 4) * 8 + h % 2 * 4 + j % 4].astype(f32), z)
        counts_out[h] = z

    def update(i, carry):
        for k in range(2):
            b = i * 2 + k
            cnt = jnp.full((1, T), jnp.maximum(su[b], 1), i32).astype(f32)
            uf[rows(b), :] = uf[rows(b), :] * KEEP + du[b] * (LR / cnt)
        return carry

    quarter = tiles // 4
    sent = []
    for part in range(4):
        lax.fori_loop(part * quarter // 2, (part + 1) * quarter // 2, update, 0)
        o = pl.ds(part * quarter * T, quarter * T)
        sent.append(pltpu.make_async_copy(uf.at[o], users_out.at[o], osem.at[part]))
        sent[-1].start()
    for cp in sent:
        cp.wait()


def tiles_step(epoch, ut, it, live, users, items, ratings, chunks=8):
    slots, T = ratings.shape[1], ratings.shape[2]
    tiles = users.shape[0] // T
    first = epoch == 0
    hbm = pl.BlockSpec(memory_space=pltpu.HBM)
    vmem = pl.BlockSpec(memory_space=pltpu.VMEM)
    smem = lambda *k: pltpu.SMEM(k, i32)
    length = slots // 2 + tiles + 2 * GROUP
    return pl.pallas_call(
        functools.partial(tile_kernel, epoch, chunks),
        out_shape=(pltpu.HBM(users.shape, f32), pltpu.VMEM((tiles, T, T), f32), pltpu.VMEM((4, 8, T), f32)),
        in_specs=[hbm] * 4 + [hbm if first else pl.BlockSpec(memory_space=pl.ANY)] + [hbm],
        out_specs=(hbm, vmem, vmem),
        scratch_shapes=[
            smem(*ut.shape), smem(*it.shape), smem(*live.shape),
            pltpu.VMEM((slots, T, T), bf16),
            pltpu.VMEM(users.shape, f32),
            pltpu.VMEM(items.shape, f32),
            pltpu.VMEM((tiles, T, T), bf16), pltpu.VMEM((tiles, T, T), bf16), pltpu.VMEM((tiles, T, T), bf16),
            pltpu.VMEM((tiles, T, T), f32),
            pltpu.VMEM((GROUP, T, 2 * T), bf16),
            smem(length), smem(length), smem(length), smem(tiles // 2), smem(tiles), smem(tiles), smem(tiles),
            pltpu.SemaphoreType.DMA((chunks,)), pltpu.SemaphoreType.DMA((5,)), pltpu.SemaphoreType.DMA((4,)),
        ],
        compiler_params=pltpu.CompilerParams(vmem_limit_bytes=32 << 20),
        name=f"tile_step_{epoch}",
    )(pin(ut), pin(it), pin(live), pin(users), pin(items) if first else items, pin(ratings))


MESH = pl.DeviceIdType.MESH


def share_kernel(mask, grads, counts, block, dest, hold, acc, old, new, rx1, ry, rx2, cin, cmine,
                 s1, r1, sy, ry_s, s2, r2, sc, rc, se, re, t2, q2, ty, qy, t1, q1, lsem, wsem):
    T = block.shape[1]
    s = lax.axis_index("stratum")
    r = lax.axis_index("replica")
    x, hy = lax.div(r, 2), lax.rem(r, 2)
    lo, hi = lax.rem(x, 2), lax.div(x, 2)
    xa = x + 1 - 2 * lo
    xb = 3 - x
    at = lambda x_, y_: (s, x_ * 2 + y_)
    first = (at(xa, hy), at(xb, hy))
    second = (at(xb, hy), at(xa, hy))
    over = at(x, 1 - hy)
    h1 = (lo + hi - 2 * lo * hi, hi)
    h2 = (lo, lo)

    def tile(d, c, a, b, e):
        return (d * 2 + c) * 8 + a * 4 + b * 2 + e

    def put(src, dst, ss, rs, dev):
        cp = pltpu.make_async_remote_copy(src_ref=src, dst_ref=dst, send_sem=ss, recv_sem=rs, device_id=dev, device_id_type=MESH)
        cp.start()
        return cp

    def rows(b):
        return pl.ds(pl.multiple_of(b * T, T), T)

    out = hold if mask else dest
    saved = []

    def save(b):
        if mask:
            saved.append(pltpu.make_async_copy(out.at[rows(b)], dest.at[rows(b)], wsem.at[len(saved)]))
            saved[-1].start()

    bar = pltpu.get_barrier_semaphore()
    for dev in (*first, over):
        pl.semaphore_signal(bar, inc=1, device_id=dev, device_id_type=MESH)
    across = s
    if mask:
        for bit in range(4):
            if mask >> bit & 1:
                across = across + (1 << bit) - (2 << bit) * lax.rem(lax.div(s, 1 << bit), 2)
        pl.semaphore_signal(bar, inc=1, device_id=(across, r), device_id_type=MESH)
    local = []
    mine = {}
    for d in range(2):
        for c in range(2):
            b = tile(d, c, h1[d], hy, h2[d])
            mine[d, c] = b
            local.append(pltpu.make_async_copy(block.at[rows(b)], old.at[d, c], lsem.at[2 + d * 2 + c]))
    for cp in local:
        cp.start()
    pl.semaphore_wait(bar, 4 if mask else 3)

    pend = []
    got1, goty, got2, gote = {}, {}, {}, {}
    def go(c, half):
        for e in range(2):
            for d in range(2):
                i = half * 2 + e
                yb = hy if half else 1 - hy
                eb = 1 - h2[d] if e else h2[d]
                got1[d, c, i] = put(grads.at[tile(d, c, 1 - h1[d], yb, eb)], rx1.at[d, c, i], s1.at[d, c, i], r1.at[d, c, i], first[d])

    gotc = [put(counts.at[d * 2 + 1 - h1[d]], cin.at[0, d], sc.at[0, d], rc.at[0, d], first[d]) for d in range(2)]
    go(0, 0)
    go(0, 1)

    def tally(step):
        for d in range(2):
            gotc[step * 2 + d].wait_recv()
            before = cmine[step - 1, d] if step else counts[d * 2 + h1[d]]
            cmine[step, d] = before + cin[step, d]
            if step < 2:
                gotc.append(put(cmine.at[step, d], cin.at[step + 1, d], sc.at[step + 1, d], rc.at[step + 1, d], second[d] if step else over))

    for cp in local:
        cp.wait()

    def add(d, c, a, b, e, part):
        t = tile(d, c, a, b, e)
        acc[t] = acc[t] + part[...]

    def take1(c, i):
        for d in range(2):
            e = h2[d] if i % 2 else 1 - h2[d]
            b = hy if i >= 2 else 1 - hy
            got1[d, c, i].wait_recv()
            t = tile(d, c, h1[d], b, e)
            acc[t] = grads[t] + rx1[d, c, i]
            if i < 2:
                goty[d, c, i] = put(acc.at[tile(d, c, h1[d], b, e)], ry.at[d, c, i], sy.at[d, c, i], ry_s.at[d, c, i], over)

    def takey(c, j):
        for d in range(2):
            e = h2[d] if j else 1 - h2[d]
            goty[d, c, j].wait_recv()
            add(d, c, h1[d], hy, e, ry.at[d, c, j])
            if j == 0:
                got2[d, c] = put(acc.at[tile(d, c, h1[d], hy, e)], rx2.at[d, c], s2.at[d, c], r2.at[d, c], second[d])

    own = {}
    def finish(c):
        for d in range(2):
            b = mine[d, c]
            got2[d, c].wait_recv()
            total = acc[b] + rx2[d, c]
            cnt = jnp.maximum(cmine[2, d, pl.ds(c * 4 + hy * 2 + h2[d], 1), :], 1.0)
            fresh = old[d, c] * KEEP + total.T * (LR / cnt)
            if mask:
                new[d, c] = fresh
                gote[d, c] = put(new.at[d, c], out.at[rows(b)], se.at[d, c], re.at[d, c], (across, r))
            else:
                out[rows(b), :] = fresh

    ag2, agy, ag1 = {}, {}, {}

    def send2(d, c, b):
        ag2[d, c] = put(out.at[rows(b)], out.at[rows(b)], t2.at[d, c], q2.at[d, c], second[d])

    def sendy(d, c, j, b):
        agy[d, c, j] = put(out.at[rows(b)], out.at[rows(b)], ty.at[d, c, j], qy.at[d, c, j], over)

    def send1(d, c, i, b):
        ag1[d, c, i] = put(out.at[rows(b)], out.at[rows(b)], t1.at[d, c, i], q1.at[d, c, i], first[d])

    def spread(c):
        for d in range(2):
            b = mine[d, c]
            if mask:
                gote[d, c].wait_recv()
            send2(d, c, b)
            sendy(d, c, 0, b)
            send1(d, c, 0, b)
            save(b)

    def pass2(c):
        for d in range(2):
            ag2[d, c].wait_recv()
            b = tile(d, c, h1[d], hy, 1 - h2[d])
            sendy(d, c, 1, b)
            send1(d, c, 1, b)
            save(b)

    def passy(c, j):
        for d in range(2):
            agy[d, c, j].wait_recv()
            b = tile(d, c, h1[d], 1 - hy, 1 - h2[d] if j else h2[d])
            send1(d, c, 2 + j, b)
            save(b)

    tally(0)
    take1(0, 0)
    take1(0, 1)
    go(1, 0)
    take1(0, 2)
    take1(0, 3)
    tally(1)
    takey(0, 0)
    go(1, 1)
    take1(1, 0)
    take1(1, 1)
    takey(0, 1)
    tally(2)
    finish(0)
    if not mask:
        spread(0)
    take1(1, 2)
    takey(1, 0)
    take1(1, 3)
    if not mask:
        pass2(0)
    takey(1, 1)
    finish(1)
    if mask:
        spread(0)
    if mask:
        pass2(0)
    spread(1)
    passy(0, 0)
    pass2(1)
    passy(0, 1)
    passy(1, 0)
    passy(1, 1)
    for c in range(2):
        for i in range(4):
            for d in range(2):
                ag1[d, c, i].wait_recv()
                save(tile(d, c, 1 - h1[d], 1 - hy if i >= 2 else hy, h2[d] if i % 2 else 1 - h2[d]))
    for table in (got1, goty, got2, gote, ag2, agy, ag1):
        for cp in table.values():
            cp.wait_send()
    for g in gotc:
        g.wait_send()
    for cp in saved:
        cp.wait()


def share(grads, counts, block, mask, cid):
    tiles, T = grads.shape[0], grads.shape[1]
    vmem = pl.BlockSpec(memory_space=pltpu.VMEM)
    hbm = pl.BlockSpec(memory_space=pltpu.HBM)
    dma = lambda *k: pltpu.SemaphoreType.DMA(k)
    both = lambda *k: [dma(*k), dma(*k)]
    return pl.pallas_call(
        functools.partial(share_kernel, mask),
        out_shape=(pltpu.HBM if mask else pltpu.VMEM)(block.shape, f32),
        in_specs=[vmem, vmem, hbm if mask else pl.BlockSpec(memory_space=pl.ANY)],
        out_specs=hbm if mask else vmem,
        scratch_shapes=[
            pltpu.VMEM(block.shape if mask else (8, T), f32),
            pltpu.VMEM((tiles, T, T), f32),
            pltpu.VMEM((2, 2, T, T), f32),
            pltpu.VMEM((2, 2, T, T), f32),
            pltpu.VMEM((2, 2, 4, T, T), f32),
            pltpu.VMEM((2, 2, 2, T, T), f32),
            pltpu.VMEM((2, 2, T, T), f32),
            pltpu.VMEM((3, 2, 8, T), f32),
            pltpu.VMEM((3, 2, 8, T), f32),
            *both(2, 2, 4), *both(2, 2, 2), *both(2, 2), *both(3, 2), *both(2, 2),
            *both(2, 2), *both(2, 2, 2), *both(2, 2, 4), dma(6), dma(tiles),
        ],
        compiler_params=pltpu.CompilerParams(collective_id=cid, has_side_effects=True, vmem_limit_bytes=24 << 20),
        name=f"share_{mask}",
    )(grads, counts, pin(block) if mask else block)


def local(user_factors, item_factors, ratings, user_tile, item_tile, live_count, partner):
    half = lax.axis_size("stratum") // 2
    live_count = live_count.reshape(-1)
    users, grads, counts = tiles_step(0, user_tile, item_tile, live_count, user_factors, item_factors, ratings)
    branches = [functools.partial(share, mask=half + k, cid=1 + k) for k in range(half)]
    block = lax.switch(partner[0] - half, branches, grads, counts, item_factors)
    users, grads, counts = tiles_step(1, user_tile, item_tile, live_count, users, block, ratings)
    return users, share(grads, counts, block, 0, 0)


def solution(mesh):
    return jax.shard_map(
        local,
        mesh=mesh,
        in_specs=(
            P(("stratum", "replica"), None),
            P("stratum", None),
            P(None, ("stratum", "replica"), None, None),
            P(None, ("stratum", "replica")),
            P(None, ("stratum", "replica")),
            P(None, ("stratum", "replica")),
            P(),
        ),
        out_specs=(P(("stratum", "replica"), None), P("stratum", None)),
        check_vma=False,
    )
```

```python
import functools

import jax
import jax.numpy as jnp
from jax import lax
from jax.experimental import pallas as pl
from jax.experimental.pallas import tpu as pltpu
from jax.sharding import PartitionSpec as P

LR = 0.05
KEEP = 1.0 - 0.05 * 0.05
NT = (((1,), (1,)), ((), ()))
NN = (((1,), (0,)), ((), ()))
f32, bf16, i32 = jnp.float32, jnp.bfloat16, jnp.int32
GROUP = 16


def pin(x, space=pltpu.HBM):
    return pltpu.with_memory_space_constraint(x, space)


def tile_kernel(epoch, chunks, ut_in, it_in, live_in, users, items, ratings,
                users_out, dv, counts_out, seen_out,
                ut, it, live_ref, rat, uf, vf, ub, utb, vb, du,
                rbuf, pa, p1, p2, nb, pend, su, si, rsem, msem, osem):
    tiles, T = ub.shape[0], ub.shape[1]
    slots = rat.shape[0]
    width = slots // chunks
    first = epoch == 0
    if first:
        du = users_out
    per = slots // tiles

    def load(c):
        o = pl.ds(c * width, width)
        return pltpu.make_async_copy(ratings.at[epoch, o], rat.at[o], rsem.at[c])

    def rows(b):
        return pl.ds(pl.multiple_of(b * T, T), T)

    small = [pltpu.make_async_copy(ut_in, ut, msem.at[0]), pltpu.make_async_copy(it_in, it, msem.at[1]),
             pltpu.make_async_copy(live_in, live_ref, msem.at[2])]
    big = [pltpu.make_async_copy(users, uf, msem.at[3]), pltpu.make_async_copy(items, vf, msem.at[4])]
    for cp in small + big:
        cp.start()
    for c in range(2):
        load(c).start()

    @pl.loop(0, tiles)
    def _(b):
        su[b] = 0
        si[b] = 0
        pend[b] = -1
        du[b] = jnp.zeros((T, T), f32)
        dv[b] = jnp.zeros((T, T), f32)

    for cp in small:
        cp.wait()
    live = live_ref[epoch]

    def pair(i, np):
        for k in range(2 * per):
            t = i * (2 * per) + k
            a, b = ut[epoch, t], it[epoch, t]
            valid = t < live
            q = pend[a]
            has = jnp.logical_and(valid, q >= 0)
            pa[np] = a
            p1[np] = q
            p2[np] = t
            np = np + has.astype(i32)
            pend[a] = jnp.where(valid, jnp.where(has, -1, t), q)
            one = valid.astype(i32)
            su[a] = su[a] + one
            si[b] = si[b] + one
        nb[i] = np
        return np

    early = tiles // 4
    pairs = lax.fori_loop(0, early, pair, jnp.int32(GROUP))
    for c in range(2, chunks):
        load(c).start()
    for cp in big:
        cp.wait()
    eye = (lax.broadcasted_iota(i32, (T, T), 0) == lax.broadcasted_iota(i32, (T, T), 1)).astype(bf16)

    def cast(i, np):
        for k in range(4):
            b = i * 4 + k
            x = uf[rows(b), :].astype(bf16)
            ub[b] = x
            utb[b] = lax.dot_general(eye, x, NT, preferred_element_type=f32).astype(bf16)
            vb[b] = vf[rows(b), :].astype(bf16)
        return pair(early + i, np)

    pairs = lax.fori_loop(0, tiles // 4, cast, pairs)

    @functools.partial(lax.fori_loop, 0, tiles, init_val=pairs)
    def total(a, np):
        q = pend[a]
        pa[np] = a
        p1[np] = q
        p2[np] = -1
        return np + (q >= 0).astype(i32)

    for k in range(GROUP):
        for o in (0, total):
            pa[o + k] = 0
            p1[o + k] = -1
            p2[o + k] = -1

    rbuf[...] = jnp.zeros(rbuf.shape, bf16)

    def names(g):
        out = []
        for k in range(GROUP):
            p = g * GROUP + k
            x, y = p1[p], p2[p]
            tx, ty = jnp.maximum(x, 0), jnp.maximum(y, 0)
            out.append((pa[p], x, y, tx, ty, it[epoch, tx], it[epoch, ty]))
        return out

    def flush(k, name):
        a, x, y, tx, ty, bx, by = name
        r = rbuf[k]
        v = jnp.concatenate([vb[bx], vb[by]], axis=0)
        gu = lax.dot_general(r, v, NN, preferred_element_type=f32)
        gv = lax.dot_general(utb[a], r, NN, preferred_element_type=f32)
        return gu, gv

    def settle(name, gu, gv):
        a, x, y, tx, ty, bx, by = name
        du[a] += gu
        dv[bx] += gv[:, :T]
        dv[by] += gv[:, T:]

    def fill(k, name):
        a, x, y, tx, ty, bx, by = name
        v = jnp.concatenate([vb[bx], vb[by]], axis=0)
        p = lax.dot_general(ub[a], v, NT, preferred_element_type=f32)
        r1 = (rat[tx].astype(f32) - p[:, :T]).astype(bf16)
        r2 = (rat[ty].astype(f32) - p[:, T:]).astype(bf16)
        zero = jnp.zeros((T, T), bf16)
        rbuf[k] = jnp.concatenate([jnp.where(x >= 0, r1, zero), jnp.where(y >= 0, r2, zero)], axis=1)

    def work(g, carry):
        now, later = names(g), names(g + 1)
        for k in range(GROUP):
            gu, gv = flush(k, now[k])
            fill(k, later[k])
            settle(now[k], gu, gv)
        return carry

    def chunk(c, done):
        load(c).wait()
        upto = nb[(c + 1) * (tiles // 2 // chunks) - 1] // GROUP - 1
        upto = jnp.where(c == chunks - 1, pl.cdiv(total, GROUP) - 1, upto)
        lax.fori_loop(done, upto, work, 0)
        return jnp.maximum(done, upto)

    ended = lax.fori_loop(0, chunks, chunk, jnp.int32(0))
    last = names(ended)
    for k in range(GROUP):
        settle(last[k], *flush(k, last[k]))

    row = lax.broadcasted_iota(i32, (8, T), 0)
    for h in range(4):
        z = jnp.zeros((8, T), f32)
        for j in range(8):
            z = jnp.where(row == j, si[(h // 2 * 2 + j // 4) * 8 + h % 2 * 4 + j % 4].astype(f32), z)
        counts_out[h] = z

    if first:
        for h in range(tiles // 8):
            z = jnp.zeros((8, T), f32)
            for j in range(8):
                z = jnp.where(row == j, jnp.maximum(su[h * 8 + j], 1).astype(f32), z)
            seen_out[pl.ds(h * 8, 8), :] = z
        return
    seen_out[...] = jnp.zeros(seen_out.shape, f32)

    def update(i, carry):
        for k in range(2):
            b = i * 2 + k
            cnt = jnp.full((1, T), jnp.maximum(su[b], 1), i32).astype(f32)
            uf[rows(b), :] = uf[rows(b), :] * KEEP + du[b] * (LR / cnt)
        return carry

    quarter = tiles // 4
    sent = []
    for part in range(4):
        lax.fori_loop(part * quarter // 2, (part + 1) * quarter // 2, update, 0)
        o = pl.ds(part * quarter * T, quarter * T)
        sent.append(pltpu.make_async_copy(uf.at[o], users_out.at[o], osem.at[part]))
        sent[-1].start()
    for cp in sent:
        cp.wait()


def tiles_step(epoch, ut, it, live, users, items, ratings, chunks=8):
    slots, T = ratings.shape[1], ratings.shape[2]
    tiles = users.shape[0] // T
    first = epoch == 0
    hbm = pl.BlockSpec(memory_space=pltpu.HBM)
    vmem = pl.BlockSpec(memory_space=pltpu.VMEM)
    smem = lambda *k: pltpu.SMEM(k, i32)
    length = slots // 2 + tiles + 2 * GROUP
    return pl.pallas_call(
        functools.partial(tile_kernel, epoch, chunks),
        out_shape=(pltpu.VMEM((tiles, T, T), f32) if first else pltpu.HBM(users.shape, f32), pltpu.VMEM((tiles, T, T), f32), pltpu.VMEM((4, 8, T), f32), pltpu.VMEM((tiles, T), f32)),
        in_specs=[hbm] * 4 + [hbm if first else pl.BlockSpec(memory_space=pl.ANY)] + [hbm],
        out_specs=(vmem if first else hbm, vmem, vmem, vmem),
        scratch_shapes=[
            smem(*ut.shape), smem(*it.shape), smem(*live.shape),
            pltpu.VMEM((slots, T, T), bf16),
            pltpu.VMEM(users.shape, f32),
            pltpu.VMEM(items.shape, f32),
            pltpu.VMEM((tiles, T, T), bf16), pltpu.VMEM((tiles, T, T), bf16), pltpu.VMEM((tiles, T, T), bf16),
            pltpu.VMEM((8, T) if first else (tiles, T, T), f32),
            pltpu.VMEM((GROUP, T, 2 * T), bf16),
            smem(length), smem(length), smem(length), smem(tiles // 2), smem(tiles), smem(tiles), smem(tiles),
            pltpu.SemaphoreType.DMA((chunks,)), pltpu.SemaphoreType.DMA((5,)), pltpu.SemaphoreType.DMA((4,)),
        ],
        compiler_params=pltpu.CompilerParams(vmem_limit_bytes=32 << 20),
        name=f"tile_step_{epoch}",
    )(pin(ut), pin(it), pin(live), pin(users), pin(items) if first else items, pin(ratings))


MESH = pl.DeviceIdType.MESH


def share_kernel(mask, grads, counts, block, *rest):
    if mask:
        users, user_grad, seen, dest, users_out, *rest, ubuf, usem, osem = rest
    else:
        dest, *rest = rest
    share_body(mask, grads, counts, block, dest, (users, user_grad, seen, users_out, ubuf, usem, osem) if mask else None, *rest)


def share_body(mask, grads, counts, block, dest, extra, hold, acc, old, new, rx1, ry, rx2, cin, cmine,
                 s1, r1, sy, ry_s, s2, r2, sc, rc, se, re, t2, q2, ty, qy, t1, q1, lsem, wsem):
    T = block.shape[1]
    s = lax.axis_index("stratum")
    r = lax.axis_index("replica")
    x, hy = lax.div(r, 2), lax.rem(r, 2)
    lo, hi = lax.rem(x, 2), lax.div(x, 2)
    xa = x + 1 - 2 * lo
    xb = 3 - x
    at = lambda x_, y_: (s, x_ * 2 + y_)
    first = (at(xa, hy), at(xb, hy))
    second = (at(xb, hy), at(xa, hy))
    over = at(x, 1 - hy)
    h1 = (lo + hi - 2 * lo * hi, hi)
    h2 = (lo, lo)

    def tile(d, c, a, b, e):
        return (d * 2 + c) * 8 + a * 4 + b * 2 + e

    def put(src, dst, ss, rs, dev):
        cp = pltpu.make_async_remote_copy(src_ref=src, dst_ref=dst, send_sem=ss, recv_sem=rs, device_id=dev, device_id_type=MESH)
        cp.start()
        return cp

    def rows(b):
        return pl.ds(pl.multiple_of(b * T, T), T)

    out = hold if mask else dest
    saved = []

    def save(b):
        if mask:
            saved.append(pltpu.make_async_copy(out.at[rows(b)], dest.at[rows(b)], wsem.at[len(saved)]))
            saved[-1].start()

    bar = pltpu.get_barrier_semaphore()
    for dev in (*first, over):
        pl.semaphore_signal(bar, inc=1, device_id=dev, device_id_type=MESH)
    across = s
    if mask:
        for bit in range(4):
            if mask >> bit & 1:
                across = across + (1 << bit) - (2 << bit) * lax.rem(lax.div(s, 1 << bit), 2)
        pl.semaphore_signal(bar, inc=1, device_id=(across, r), device_id_type=MESH)
    local = []
    parts = []
    if mask:
        users, user_grad, seen, users_out, ubuf, usem, osem = extra
        fetch = pltpu.make_async_copy(users, ubuf, usem)
        fetch.start()
    quarter = grads.shape[0] // 4

    def improve(part):
        if not mask:
            return

        @pl.loop(part * quarter, (part + 1) * quarter)
        def _(b):
            ubuf[rows(b), :] = ubuf[rows(b), :] * KEEP + user_grad[b] * (LR / seen[pl.ds(b, 1), :])

        o = pl.ds(part * quarter * T, quarter * T)
        parts.append(pltpu.make_async_copy(ubuf.at[o], users_out.at[o], osem.at[part]))
        parts[-1].start()

    mine = {}
    for d in range(2):
        for c in range(2):
            b = tile(d, c, h1[d], hy, h2[d])
            mine[d, c] = b
            local.append(pltpu.make_async_copy(block.at[rows(b)], old.at[d, c], lsem.at[2 + d * 2 + c]))
    for cp in local:
        cp.start()
    pl.semaphore_wait(bar, 4 if mask else 3)

    pend = []
    got1, goty, got2, gote = {}, {}, {}, {}
    def go(c, half):
        for e in range(2):
            for d in range(2):
                i = half * 2 + e
                yb = hy if half else 1 - hy
                eb = 1 - h2[d] if e else h2[d]
                got1[d, c, i] = put(grads.at[tile(d, c, 1 - h1[d], yb, eb)], rx1.at[d, c, i], s1.at[d, c, i], r1.at[d, c, i], first[d])

    gotc = [put(counts.at[d * 2 + 1 - h1[d]], cin.at[0, d], sc.at[0, d], rc.at[0, d], first[d]) for d in range(2)]
    go(0, 0)
    go(0, 1)

    def tally(step):
        for d in range(2):
            gotc[step * 2 + d].wait_recv()
            before = cmine[step - 1, d] if step else counts[d * 2 + h1[d]]
            cmine[step, d] = before + cin[step, d]
            if step < 2:
                gotc.append(put(cmine.at[step, d], cin.at[step + 1, d], sc.at[step + 1, d], rc.at[step + 1, d], second[d] if step else over))

    for cp in local:
        cp.wait()

    def add(d, c, a, b, e, part):
        t = tile(d, c, a, b, e)
        acc[t] = acc[t] + part[...]

    def take1(c, i):
        for d in range(2):
            e = h2[d] if i % 2 else 1 - h2[d]
            b = hy if i >= 2 else 1 - hy
            got1[d, c, i].wait_recv()
            t = tile(d, c, h1[d], b, e)
            acc[t] = grads[t] + rx1[d, c, i]
            if i < 2:
                goty[d, c, i] = put(acc.at[tile(d, c, h1[d], b, e)], ry.at[d, c, i], sy.at[d, c, i], ry_s.at[d, c, i], over)

    def takey(c, j):
        for d in range(2):
            e = h2[d] if j else 1 - h2[d]
            goty[d, c, j].wait_recv()
            add(d, c, h1[d], hy, e, ry.at[d, c, j])
            if j == 0:
                got2[d, c] = put(acc.at[tile(d, c, h1[d], hy, e)], rx2.at[d, c], s2.at[d, c], r2.at[d, c], second[d])

    own = {}
    def finish(c):
        for d in range(2):
            b = mine[d, c]
            got2[d, c].wait_recv()
            total = acc[b] + rx2[d, c]
            cnt = jnp.maximum(cmine[2, d, pl.ds(c * 4 + hy * 2 + h2[d], 1), :], 1.0)
            fresh = old[d, c] * KEEP + total.T * (LR / cnt)
            if mask:
                new[d, c] = fresh
                gote[d, c] = put(new.at[d, c], out.at[rows(b)], se.at[d, c], re.at[d, c], (across, r))
            else:
                out[rows(b), :] = fresh

    ag2, agy, ag1 = {}, {}, {}

    def send2(d, c, b):
        ag2[d, c] = put(out.at[rows(b)], out.at[rows(b)], t2.at[d, c], q2.at[d, c], second[d])

    def sendy(d, c, j, b):
        agy[d, c, j] = put(out.at[rows(b)], out.at[rows(b)], ty.at[d, c, j], qy.at[d, c, j], over)

    def send1(d, c, i, b):
        ag1[d, c, i] = put(out.at[rows(b)], out.at[rows(b)], t1.at[d, c, i], q1.at[d, c, i], first[d])

    def spread(c):
        for d in range(2):
            b = mine[d, c]
            if mask:
                gote[d, c].wait_recv()
            send2(d, c, b)
            sendy(d, c, 0, b)
            send1(d, c, 0, b)
            save(b)

    def pass2(c):
        for d in range(2):
            ag2[d, c].wait_recv()
            b = tile(d, c, h1[d], hy, 1 - h2[d])
            sendy(d, c, 1, b)
            send1(d, c, 1, b)
            save(b)

    def passy(c, j):
        for d in range(2):
            agy[d, c, j].wait_recv()
            b = tile(d, c, h1[d], 1 - hy, 1 - h2[d] if j else h2[d])
            send1(d, c, 2 + j, b)
            save(b)

    tally(0)
    take1(0, 0)
    take1(0, 1)
    go(1, 0)
    take1(0, 2)
    take1(0, 3)
    tally(1)
    takey(0, 0)
    go(1, 1)
    take1(1, 0)
    take1(1, 1)
    takey(0, 1)
    tally(2)
    finish(0)
    if not mask:
        spread(0)
    take1(1, 2)
    if mask:
        fetch.wait()
    improve(0)
    takey(1, 0)
    take1(1, 3)
    if not mask:
        pass2(0)
    takey(1, 1)
    finish(1)
    improve(1)
    if mask:
        spread(0)
    if mask:
        pass2(0)
    spread(1)
    passy(0, 0)
    improve(2)
    pass2(1)
    passy(0, 1)
    improve(3)
    passy(1, 0)
    passy(1, 1)
    for c in range(2):
        for i in range(4):
            for d in range(2):
                ag1[d, c, i].wait_recv()
                save(tile(d, c, 1 - h1[d], 1 - hy if i >= 2 else hy, h2[d] if i % 2 else 1 - h2[d]))
    for table in (got1, goty, got2, gote, ag2, agy, ag1):
        for cp in table.values():
            cp.wait_send()
    for g in gotc:
        g.wait_send()
    for cp in saved + parts:
        cp.wait()


def share(grads, counts, block, *more, mask, cid):
    tiles, T = grads.shape[0], grads.shape[1]
    vmem = pl.BlockSpec(memory_space=pltpu.VMEM)
    hbm = pl.BlockSpec(memory_space=pltpu.HBM)
    dma = lambda *k: pltpu.SemaphoreType.DMA(k)
    both = lambda *k: [dma(*k), dma(*k)]
    return pl.pallas_call(
        functools.partial(share_kernel, mask),
        out_shape=(pltpu.HBM(block.shape, f32),) * 2 if mask else pltpu.VMEM(block.shape, f32),
        in_specs=[vmem, vmem, hbm if mask else pl.BlockSpec(memory_space=pl.ANY)] + ([hbm, vmem, vmem] if mask else []),
        out_specs=(hbm, hbm) if mask else vmem,
        scratch_shapes=[
            pltpu.VMEM(block.shape if mask else (8, T), f32),
            pltpu.VMEM((tiles, T, T), f32),
            pltpu.VMEM((2, 2, T, T), f32),
            pltpu.VMEM((2, 2, T, T), f32),
            pltpu.VMEM((2, 2, 4, T, T), f32),
            pltpu.VMEM((2, 2, 2, T, T), f32),
            pltpu.VMEM((2, 2, T, T), f32),
            pltpu.VMEM((3, 2, 8, T), f32),
            pltpu.VMEM((3, 2, 8, T), f32),
            *both(2, 2, 4), *both(2, 2, 2), *both(2, 2), *both(3, 2), *both(2, 2),
            *both(2, 2), *both(2, 2, 2), *both(2, 2, 4), dma(6), dma(tiles),
            *([pltpu.VMEM(block.shape, f32), pltpu.SemaphoreType.DMA, dma(4)] if mask else []),
        ],
        compiler_params=pltpu.CompilerParams(collective_id=cid, has_side_effects=True, vmem_limit_bytes=24 << 20),
        name=f"share_{mask}",
    )(grads, counts, pin(block) if mask else block, *((pin(more[0]), *more[1:]) if mask else ()))


def local(user_factors, item_factors, ratings, user_tile, item_tile, live_count, partner):
    half = lax.axis_size("stratum") // 2
    live_count = live_count.reshape(-1)
    user_grad, grads, counts, seen = tiles_step(0, user_tile, item_tile, live_count, user_factors, item_factors, ratings)
    branches = [functools.partial(share, mask=half + k, cid=1 + k) for k in range(half)]
    block, users = lax.switch(partner[0] - half, branches, grads, counts, item_factors, user_factors, user_grad, seen)
    users, grads, counts, _ = tiles_step(1, user_tile, item_tile, live_count, users, block, ratings)
    return users, share(grads, counts, block, mask=0, cid=0)


def solution(mesh):
    return jax.shard_map(
        local,
        mesh=mesh,
        in_specs=(
            P(("stratum", "replica"), None),
            P("stratum", None),
            P(None, ("stratum", "replica"), None, None),
            P(None, ("stratum", "replica")),
            P(None, ("stratum", "replica")),
            P(None, ("stratum", "replica")),
            P(),
        ),
        out_specs=(P(("stratum", "replica"), None), P("stratum", None)),
        check_vma=False,
    )
```

```python
import functools

import jax
import jax.numpy as jnp
from jax import lax
from jax.experimental import pallas as pl
from jax.experimental.pallas import tpu as pltpu
from jax.sharding import PartitionSpec as P

LR = 0.05
KEEP = 1.0 - 0.05 * 0.05
NT = (((1,), (1,)), ((), ()))
NN = (((1,), (0,)), ((), ()))
f32, bf16, i32 = jnp.float32, jnp.bfloat16, jnp.int32
GROUP = 20


def pin(x, space=pltpu.HBM):
    return pltpu.with_memory_space_constraint(x, space)


def tile_kernel(epoch, chunks, ut_in, it_in, live_in, users, items, ratings,
                users_out, dv, counts_out, seen_out,
                ut, it, live_ref, rat, uf, vf, ub, utb, vb, du,
                rbuf, pa, p1, p2, nb, pend, su, si, rsem, msem, osem):
    tiles, T = ub.shape[0], ub.shape[1]
    slots = rat.shape[0]
    width = slots // chunks
    first = epoch == 0
    if first:
        du = users_out
    per = slots // tiles

    def load(c):
        o = pl.ds(c * width, width)
        return pltpu.make_async_copy(ratings.at[epoch, o], rat.at[o], rsem.at[c])

    def rows(b):
        return pl.ds(pl.multiple_of(b * T, T), T)

    small = [pltpu.make_async_copy(ut_in, ut, msem.at[0]), pltpu.make_async_copy(it_in, it, msem.at[1]),
             pltpu.make_async_copy(live_in, live_ref, msem.at[2])]
    big = [pltpu.make_async_copy(users, uf, msem.at[3]), pltpu.make_async_copy(items, vf, msem.at[4])]
    for cp in small + big:
        cp.start()
    for c in range(2):
        load(c).start()

    @pl.loop(0, tiles)
    def _(b):
        su[b] = 0
        si[b] = 0
        pend[b] = -1
        du[b] = jnp.zeros((T, T), f32)
        dv[b] = jnp.zeros((T, T), f32)

    for cp in small:
        cp.wait()
    live = live_ref[epoch]

    def pair(i, np):
        for k in range(2 * per):
            t = i * (2 * per) + k
            a, b = ut[epoch, t], it[epoch, t]
            valid = t < live
            q = pend[a]
            has = jnp.logical_and(valid, q >= 0)
            pa[np] = a
            p1[np] = q
            p2[np] = t
            np = np + has.astype(i32)
            pend[a] = jnp.where(valid, jnp.where(has, -1, t), q)
            one = valid.astype(i32)
            su[a] = su[a] + one
            si[b] = si[b] + one
        nb[i] = np
        return np

    early = tiles // 4
    pairs = lax.fori_loop(0, early, pair, jnp.int32(GROUP))
    for c in range(2, chunks):
        load(c).start()
    for cp in big:
        cp.wait()
    eye = (lax.broadcasted_iota(i32, (T, T), 0) == lax.broadcasted_iota(i32, (T, T), 1)).astype(bf16)

    def cast(i, np):
        for k in range(4):
            b = i * 4 + k
            x = uf[rows(b), :].astype(bf16)
            ub[b] = x
            utb[b] = lax.dot_general(eye, x, NT, preferred_element_type=f32).astype(bf16)
            vb[b] = vf[rows(b), :].astype(bf16)
        return pair(early + i, np)

    pairs = lax.fori_loop(0, tiles // 4, cast, pairs)

    @functools.partial(lax.fori_loop, 0, tiles, init_val=pairs)
    def total(a, np):
        q = pend[a]
        pa[np] = a
        p1[np] = q
        p2[np] = -1
        return np + (q >= 0).astype(i32)

    for k in range(GROUP):
        for o in (0, total):
            pa[o + k] = 0
            p1[o + k] = -1
            p2[o + k] = -1

    rbuf[...] = jnp.zeros(rbuf.shape, bf16)

    def names(g):
        out = []
        for k in range(GROUP):
            p = g * GROUP + k
            x, y = p1[p], p2[p]
            tx, ty = jnp.maximum(x, 0), jnp.maximum(y, 0)
            out.append((pa[p], x, y, tx, ty, it[epoch, tx], it[epoch, ty]))
        return out

    def flush(k, name):
        a, x, y, tx, ty, bx, by = name
        r = rbuf[k]
        v = jnp.concatenate([vb[bx], vb[by]], axis=0)
        gu = lax.dot_general(r, v, NN, preferred_element_type=f32)
        gv = lax.dot_general(utb[a], r, NN, preferred_element_type=f32)
        return gu, gv

    def settle(name, gu, gv):
        a, x, y, tx, ty, bx, by = name
        du[a] += gu
        dv[bx] += gv[:, :T]
        dv[by] += gv[:, T:]

    def fill(k, name):
        a, x, y, tx, ty, bx, by = name
        v = jnp.concatenate([vb[bx], vb[by]], axis=0)
        p = lax.dot_general(ub[a], v, NT, preferred_element_type=f32)
        r1 = (rat[tx].astype(f32) - p[:, :T]).astype(bf16)
        r2 = (rat[ty].astype(f32) - p[:, T:]).astype(bf16)
        zero = jnp.zeros((T, T), bf16)
        rbuf[k] = jnp.concatenate([jnp.where(x >= 0, r1, zero), jnp.where(y >= 0, r2, zero)], axis=1)

    def work(g, carry):
        now, later = names(g), names(g + 1)
        for k in range(GROUP):
            gu, gv = flush(k, now[k])
            fill(k, later[k])
            settle(now[k], gu, gv)
        return carry

    def chunk(c, done):
        load(c).wait()
        upto = nb[(c + 1) * (tiles // 2 // chunks) - 1] // GROUP - 1
        upto = jnp.where(c == chunks - 1, pl.cdiv(total, GROUP) - 1, upto)
        lax.fori_loop(done, upto, work, 0)
        return jnp.maximum(done, upto)

    ended = lax.fori_loop(0, chunks, chunk, jnp.int32(0))
    last = names(ended)
    for k in range(GROUP):
        settle(last[k], *flush(k, last[k]))

    row = lax.broadcasted_iota(i32, (8, T), 0)
    for h in range(4):
        z = jnp.zeros((8, T), f32)
        for j in range(8):
            z = jnp.where(row == j, si[(h // 2 * 2 + j // 4) * 8 + h % 2 * 4 + j % 4].astype(f32), z)
        counts_out[h] = z

    if first:
        for h in range(tiles // 8):
            z = jnp.zeros((8, T), f32)
            for j in range(8):
                z = jnp.where(row == j, jnp.maximum(su[h * 8 + j], 1).astype(f32), z)
            seen_out[pl.ds(h * 8, 8), :] = z
        return
    seen_out[...] = jnp.zeros(seen_out.shape, f32)

    def update(i, carry):
        for k in range(2):
            b = i * 2 + k
            cnt = jnp.full((1, T), jnp.maximum(su[b], 1), i32).astype(f32)
            uf[rows(b), :] = uf[rows(b), :] * KEEP + du[b] * (LR / cnt)
        return carry

    quarter = tiles // 4
    sent = []
    for part in range(4):
        lax.fori_loop(part * quarter // 2, (part + 1) * quarter // 2, update, 0)
        o = pl.ds(part * quarter * T, quarter * T)
        sent.append(pltpu.make_async_copy(uf.at[o], users_out.at[o], osem.at[part]))
        sent[-1].start()
    for cp in sent:
        cp.wait()


def tiles_step(epoch, ut, it, live, users, items, ratings, chunks=8):
    slots, T = ratings.shape[1], ratings.shape[2]
    tiles = users.shape[0] // T
    first = epoch == 0
    hbm = pl.BlockSpec(memory_space=pltpu.HBM)
    vmem = pl.BlockSpec(memory_space=pltpu.VMEM)
    smem = lambda *k: pltpu.SMEM(k, i32)
    length = slots // 2 + tiles + 2 * GROUP
    return pl.pallas_call(
        functools.partial(tile_kernel, epoch, chunks),
        out_shape=(pltpu.VMEM((tiles, T, T), f32) if first else pltpu.HBM(users.shape, f32), pltpu.VMEM((tiles, T, T), f32), pltpu.VMEM((4, 8, T), f32), pltpu.VMEM((tiles, T), f32)),
        in_specs=[hbm] * 4 + [hbm if first else pl.BlockSpec(memory_space=pl.ANY)] + [hbm],
        out_specs=(vmem if first else hbm, vmem, vmem, vmem),
        scratch_shapes=[
            smem(*ut.shape), smem(*it.shape), smem(*live.shape),
            pltpu.VMEM((slots, T, T), bf16),
            pltpu.VMEM(users.shape, f32),
            pltpu.VMEM(items.shape, f32),
            pltpu.VMEM((tiles, T, T), bf16), pltpu.VMEM((tiles, T, T), bf16), pltpu.VMEM((tiles, T, T), bf16),
            pltpu.VMEM((8, T) if first else (tiles, T, T), f32),
            pltpu.VMEM((GROUP, T, 2 * T), bf16),
            smem(length), smem(length), smem(length), smem(tiles // 2), smem(tiles), smem(tiles), smem(tiles),
            pltpu.SemaphoreType.DMA((chunks,)), pltpu.SemaphoreType.DMA((5,)), pltpu.SemaphoreType.DMA((4,)),
        ],
        compiler_params=pltpu.CompilerParams(vmem_limit_bytes=32 << 20),
        name=f"tile_step_{epoch}",
    )(pin(ut), pin(it), pin(live), pin(users), pin(items) if first else items, pin(ratings))


MESH = pl.DeviceIdType.MESH


def share_kernel(mask, grads, counts, block, *rest):
    if mask:
        users, user_grad, seen, dest, users_out, *rest, ubuf, usem, osem = rest
    else:
        dest, *rest = rest
    share_body(mask, grads, counts, block, dest, (users, user_grad, seen, users_out, ubuf, usem, osem) if mask else None, *rest)


def share_body(mask, grads, counts, block, dest, extra, hold, acc, old, new, rx1, ry, rx2, cin, cmine,
                 s1, r1, sy, ry_s, s2, r2, sc, rc, se, re, t2, q2, ty, qy, t1, q1, lsem, wsem):
    T = block.shape[1]
    s = lax.axis_index("stratum")
    r = lax.axis_index("replica")
    x, hy = lax.div(r, 2), lax.rem(r, 2)
    lo, hi = lax.rem(x, 2), lax.div(x, 2)
    xa = x + 1 - 2 * lo
    xb = 3 - x
    at = lambda x_, y_: (s, x_ * 2 + y_)
    first = (at(xa, hy), at(xb, hy))
    second = (at(xb, hy), at(xa, hy))
    over = at(x, 1 - hy)
    h1 = (lo + hi - 2 * lo * hi, hi)
    h2 = (lo, lo)

    def tile(d, c, a, b, e):
        return (d * 2 + c) * 8 + a * 4 + b * 2 + e

    def put(src, dst, ss, rs, dev):
        cp = pltpu.make_async_remote_copy(src_ref=src, dst_ref=dst, send_sem=ss, recv_sem=rs, device_id=dev, device_id_type=MESH)
        cp.start()
        return cp

    def rows(b):
        return pl.ds(pl.multiple_of(b * T, T), T)

    out = hold if mask else dest
    saved = []

    def save(b):
        if mask:
            saved.append(pltpu.make_async_copy(out.at[rows(b)], dest.at[rows(b)], wsem.at[len(saved)]))
            saved[-1].start()

    bar = pltpu.get_barrier_semaphore()
    for dev in (*first, over):
        pl.semaphore_signal(bar, inc=1, device_id=dev, device_id_type=MESH)
    across = s
    if mask:
        for bit in range(4):
            if mask >> bit & 1:
                across = across + (1 << bit) - (2 << bit) * lax.rem(lax.div(s, 1 << bit), 2)
        pl.semaphore_signal(bar, inc=1, device_id=(across, r), device_id_type=MESH)
    local = []
    parts = []
    if mask:
        users, user_grad, seen, users_out, ubuf, usem, osem = extra
        fetch = pltpu.make_async_copy(users, ubuf, usem)
        fetch.start()
    quarter = grads.shape[0] // 4

    def improve(part):
        if not mask:
            return

        @pl.loop(part * quarter, (part + 1) * quarter)
        def _(b):
            ubuf[rows(b), :] = ubuf[rows(b), :] * KEEP + user_grad[b] * (LR / seen[pl.ds(b, 1), :])

        o = pl.ds(part * quarter * T, quarter * T)
        parts.append(pltpu.make_async_copy(ubuf.at[o], users_out.at[o], osem.at[part]))
        parts[-1].start()

    mine = {}
    for d in range(2):
        for c in range(2):
            b = tile(d, c, h1[d], hy, h2[d])
            mine[d, c] = b
            local.append(pltpu.make_async_copy(block.at[rows(b)], old.at[d, c], lsem.at[2 + d * 2 + c]))
    for cp in local:
        cp.start()
    pl.semaphore_wait(bar, 4 if mask else 3)

    pend = []
    got1, goty, got2, gote = {}, {}, {}, {}
    def go(c, half):
        for e in range(2):
            for d in range(2):
                i = half * 2 + e
                yb = hy if half else 1 - hy
                eb = 1 - h2[d] if e else h2[d]
                got1[d, c, i] = put(grads.at[tile(d, c, 1 - h1[d], yb, eb)], rx1.at[d, c, i], s1.at[d, c, i], r1.at[d, c, i], first[d])

    gotc = [put(counts.at[d * 2 + 1 - h1[d]], cin.at[0, d], sc.at[0, d], rc.at[0, d], first[d]) for d in range(2)]
    go(0, 0)
    go(0, 1)

    def tally(step):
        for d in range(2):
            gotc[step * 2 + d].wait_recv()
            before = cmine[step - 1, d] if step else counts[d * 2 + h1[d]]
            cmine[step, d] = before + cin[step, d]
            if step < 2:
                gotc.append(put(cmine.at[step, d], cin.at[step + 1, d], sc.at[step + 1, d], rc.at[step + 1, d], second[d] if step else over))

    for cp in local:
        cp.wait()

    def add(d, c, a, b, e, part):
        t = tile(d, c, a, b, e)
        acc[t] = acc[t] + part[...]

    def take1(c, i):
        for d in range(2):
            e = h2[d] if i % 2 else 1 - h2[d]
            b = hy if i >= 2 else 1 - hy
            got1[d, c, i].wait_recv()
            t = tile(d, c, h1[d], b, e)
            acc[t] = grads[t] + rx1[d, c, i]
            if i < 2:
                goty[d, c, i] = put(acc.at[tile(d, c, h1[d], b, e)], ry.at[d, c, i], sy.at[d, c, i], ry_s.at[d, c, i], over)

    def takey(c, j):
        for d in range(2):
            e = h2[d] if j else 1 - h2[d]
            goty[d, c, j].wait_recv()
            add(d, c, h1[d], hy, e, ry.at[d, c, j])
            if j == 0:
                got2[d, c] = put(acc.at[tile(d, c, h1[d], hy, e)], rx2.at[d, c], s2.at[d, c], r2.at[d, c], second[d])

    own = {}
    def finish(c):
        for d in range(2):
            b = mine[d, c]
            got2[d, c].wait_recv()
            total = acc[b] + rx2[d, c]
            cnt = jnp.maximum(cmine[2, d, pl.ds(c * 4 + hy * 2 + h2[d], 1), :], 1.0)
            fresh = old[d, c] * KEEP + total.T * (LR / cnt)
            if mask:
                new[d, c] = fresh
                gote[d, c] = put(new.at[d, c], out.at[rows(b)], se.at[d, c], re.at[d, c], (across, r))
            else:
                out[rows(b), :] = fresh

    ag2, agy, ag1 = {}, {}, {}

    def send2(d, c, b):
        ag2[d, c] = put(out.at[rows(b)], out.at[rows(b)], t2.at[d, c], q2.at[d, c], second[d])

    def sendy(d, c, j, b):
        agy[d, c, j] = put(out.at[rows(b)], out.at[rows(b)], ty.at[d, c, j], qy.at[d, c, j], over)

    def send1(d, c, i, b):
        ag1[d, c, i] = put(out.at[rows(b)], out.at[rows(b)], t1.at[d, c, i], q1.at[d, c, i], first[d])

    def spread(c):
        for d in range(2):
            b = mine[d, c]
            if mask:
                gote[d, c].wait_recv()
            send2(d, c, b)
            sendy(d, c, 0, b)
            send1(d, c, 0, b)
            save(b)

    def pass2(c):
        for d in range(2):
            ag2[d, c].wait_recv()
            b = tile(d, c, h1[d], hy, 1 - h2[d])
            sendy(d, c, 1, b)
            send1(d, c, 1, b)
            save(b)

    def passy(c, j):
        for d in range(2):
            agy[d, c, j].wait_recv()
            b = tile(d, c, h1[d], 1 - hy, 1 - h2[d] if j else h2[d])
            send1(d, c, 2 + j, b)
            save(b)

    tally(0)
    take1(0, 0)
    take1(0, 1)
    go(1, 0)
    take1(0, 2)
    take1(0, 3)
    tally(1)
    takey(0, 0)
    go(1, 1)
    take1(1, 0)
    take1(1, 1)
    takey(0, 1)
    tally(2)
    finish(0)
    if not mask:
        spread(0)
    take1(1, 2)
    if mask:
        fetch.wait()
    improve(0)
    takey(1, 0)
    take1(1, 3)
    if not mask:
        pass2(0)
    if mask and not mask & 2:
        spread(0)
    takey(1, 1)
    finish(1)
    improve(1)
    if mask & 2:
        spread(0)
    if mask:
        pass2(0)
    spread(1)
    passy(0, 0)
    improve(2)
    pass2(1)
    passy(0, 1)
    improve(3)
    passy(1, 0)
    passy(1, 1)
    for c in range(2):
        for i in range(4):
            for d in range(2):
                ag1[d, c, i].wait_recv()
                save(tile(d, c, 1 - h1[d], 1 - hy if i >= 2 else hy, h2[d] if i % 2 else 1 - h2[d]))
    for table in (got1, goty, got2, gote, ag2, agy, ag1):
        for cp in table.values():
            cp.wait_send()
    for g in gotc:
        g.wait_send()
    for cp in saved + parts:
        cp.wait()


def share(grads, counts, block, *more, mask, cid):
    tiles, T = grads.shape[0], grads.shape[1]
    vmem = pl.BlockSpec(memory_space=pltpu.VMEM)
    hbm = pl.BlockSpec(memory_space=pltpu.HBM)
    dma = lambda *k: pltpu.SemaphoreType.DMA(k)
    both = lambda *k: [dma(*k), dma(*k)]
    return pl.pallas_call(
        functools.partial(share_kernel, mask),
        out_shape=(pltpu.HBM(block.shape, f32),) * 2 if mask else pltpu.VMEM(block.shape, f32),
        in_specs=[vmem, vmem, hbm if mask else pl.BlockSpec(memory_space=pl.ANY)] + ([hbm, vmem, vmem] if mask else []),
        out_specs=(hbm, hbm) if mask else vmem,
        scratch_shapes=[
            pltpu.VMEM(block.shape if mask else (8, T), f32),
            pltpu.VMEM((tiles, T, T), f32),
            pltpu.VMEM((2, 2, T, T), f32),
            pltpu.VMEM((2, 2, T, T), f32),
            pltpu.VMEM((2, 2, 4, T, T), f32),
            pltpu.VMEM((2, 2, 2, T, T), f32),
            pltpu.VMEM((2, 2, T, T), f32),
            pltpu.VMEM((3, 2, 8, T), f32),
            pltpu.VMEM((3, 2, 8, T), f32),
            *both(2, 2, 4), *both(2, 2, 2), *both(2, 2), *both(3, 2), *both(2, 2),
            *both(2, 2), *both(2, 2, 2), *both(2, 2, 4), dma(6), dma(tiles),
            *([pltpu.VMEM(block.shape, f32), pltpu.SemaphoreType.DMA, dma(4)] if mask else []),
        ],
        compiler_params=pltpu.CompilerParams(collective_id=cid, has_side_effects=True, vmem_limit_bytes=24 << 20),
        name=f"share_{mask}",
    )(grads, counts, pin(block) if mask else block, *((pin(more[0]), *more[1:]) if mask else ()))


def local(user_factors, item_factors, ratings, user_tile, item_tile, live_count, partner):
    half = lax.axis_size("stratum") // 2
    live_count = live_count.reshape(-1)
    user_grad, grads, counts, seen = tiles_step(0, user_tile, item_tile, live_count, user_factors, item_factors, ratings)
    branches = [functools.partial(share, mask=half + k, cid=1 + k) for k in range(half)]
    block, users = lax.switch(partner[0] - half, branches, grads, counts, item_factors, user_factors, user_grad, seen)
    users, grads, counts, _ = tiles_step(1, user_tile, item_tile, live_count, users, block, ratings)
    return users, share(grads, counts, block, mask=0, cid=0)


def solution(mesh):
    return jax.shard_map(
        local,
        mesh=mesh,
        in_specs=(
            P(("stratum", "replica"), None),
            P("stratum", None),
            P(None, ("stratum", "replica"), None, None),
            P(None, ("stratum", "replica")),
            P(None, ("stratum", "replica")),
            P(None, ("stratum", "replica")),
            P(),
        ),
        out_specs=(P(("stratum", "replica"), None), P("stratum", None)),
        check_vma=False,
    )
```
